32 devices in a mesh: layer: 4 (over x, core), feat: 8 (over z, y).
Axes of the slice: x: 2, y: 2, z: 4, core: 2. Of those that a mesh axis runs over, the one named last changes fastest.
Arguments:
- gradient: bfloat16 [4, 2560, 2560], P('layer', 'feat'), may hold values from -3 to 3
- in_inverse: bfloat16 [4, 2560, 2560], P('layer', 'feat'), may hold values from -1 to 2.5, as said below
- in_coupling: bfloat16 [4, 2560, 2560], P('layer', 'feat'), may hold values from -0.125 to 0.125
- in_carry: bfloat16 [4, 2560, 2560], P('layer', 'feat'), may hold values from -0.125 to 0.125
- out_inverse: bfloat16 [4, 20, 128, 128], P('layer'), may hold values from -1 to 2.5, as said below
- out_coupling: bfloat16 [4, 20, 128, 128], P('layer'), may hold values from -0.5 to 0.5
Outputs:
- update: bfloat16 [4, 2560, 2560], P('layer', 'feat')
The draws below stay inside these ranges and needn't reach their ends.
Inputs may be any that keep to these rules, and one draw needn't show every extreme that they name: `in_inverse`: symmetric in its last two dimensions. `out_inverse`: symmetric in its last two dimensions.
All inputs are finite; a program needn't handle non-finite values.
Results may differ from the reference program's by a relative error of at most 0.006.
Values may be sent and summed in bfloat16 or wider, within the bound.
A program may use at most 64 MiB of HBM per device.

```python
import math
import jax
import jax.numpy as jnp
from jax import lax

DIN = 2560
DOUT = 2560
BLK = 128
LAYERS = 4
OBLOCKS = 20


def symmetric_blocks(key, leading, matrix_order, spread, lower_end, upper_end):
    first_key, second_key = jax.random.split(key)
    noise_part = jax.random.truncated_normal(first_key, -4.0, 4.0, leading + (matrix_order, matrix_order), jnp.float32)
    off_part = (noise_part + jnp.swapaxes(noise_part, -1, -2)) * (spread / math.sqrt(2.0 * matrix_order))
    diagonal = jax.random.uniform(second_key, leading + (matrix_order,), jnp.float32, lower_end, upper_end)
    identity = jnp.eye(matrix_order, dtype=jnp.float32)
    return off_part * (1.0 - identity) + diagonal[..., None] * identity


def draw_in_inverse(key, part):
    matrix = symmetric_blocks(jax.random.fold_in(key, 11), (LAYERS,), DIN, 0.45, 1.0, 2.0)
    return matrix.astype(jnp.bfloat16)


def draw_out_inverse(key, part):
    matrix = symmetric_blocks(jax.random.fold_in(key, 23), (LAYERS, DOUT // BLK), BLK, 0.45, 1.0, 2.0)
    return matrix.astype(jnp.bfloat16)


def level_of(rng, dims, cuts, smallest, top_value):
    loudness, own = 1.0, jax.random.fold_in(rng, 6)
    for axis_at, shards_of in cuts:
        draws = jnp.exp(jax.random.uniform(jax.random.fold_in(own, axis_at), (shards_of,), jnp.float32, smallest / len(cuts), top_value / len(cuts)))
        loudness = loudness * jnp.repeat(draws, dims[axis_at] // shards_of).reshape([-1 if axis == axis_at else 1 for axis in range(len(dims))])
    return loudness


def noise(key, dims, width, limit, shards=(), kind=jnp.bfloat16):
    loudness = level_of(key, dims, shards, -0.22, 0.18) if shards else 1.0
    entries = jax.random.normal(key, dims, jnp.float32) * width * loudness
    return jnp.minimum(jnp.maximum(entries, -limit), limit).astype(kind)


def setup_inputs(seed: int = 0) -> dict:
    key_list = jax.random.split(jax.random.key(seed), 7)
    gradient = noise(key_list[0], (LAYERS, DIN, DOUT), 0.5, 3.0, ((0, 4), (1, 8)))
    in_inverse = draw_in_inverse(jax.random.fold_in(key_list[6], 71), 0)
    in_coupling = noise(key_list[2], (LAYERS, DIN, DIN), DIN ** -0.5, 0.125, ((0, 4), (1, 8)))
    in_carry = noise(key_list[3], (LAYERS, DIN, DIN), DIN ** -0.5, 0.125, ((0, 4), (1, 8)))
    out_inverse = draw_out_inverse(jax.random.fold_in(key_list[6], 71), 0)
    out_coupling = noise(key_list[5], (LAYERS, OBLOCKS, BLK, BLK), BLK ** -0.5, 0.5, ((0, 4),))
    return {"gradient": gradient, "in_inverse": in_inverse, "in_coupling": in_coupling, "in_carry": in_carry, "out_inverse": out_inverse, "out_coupling": out_coupling}


def block_apply(matrix, table, flipped):
    row_count = matrix.shape[0]
    blocks = table.shape[0]
    block_width = table.shape[1]
    grouped = matrix.astype(jnp.float32).reshape(row_count, blocks, block_width)
    pattern = "rnb,ncb->rnc" if flipped else "rnb,nbc->rnc"
    product = jnp.einsum(pattern, grouped, table.astype(jnp.float32), precision=lax.Precision.HIGHEST)
    return product.reshape(row_count, blocks * block_width)


def reference(gradient, in_inverse, in_coupling, in_carry, out_inverse, out_coupling):
    results = []
    pushed_prev = jnp.zeros((DIN, DOUT), jnp.float32)
    for position in range(LAYERS):
        if position + 1 < LAYERS:
            near_rows = block_apply(gradient[position + 1], out_coupling[position], True).astype(jnp.bfloat16)
            coupled = jnp.dot(in_coupling[position], near_rows, preferred_element_type=jnp.float32)
        else:
            coupled = jnp.zeros((DIN, DOUT), jnp.float32)
        reduced = (gradient[position].astype(jnp.float32) - coupled).astype(jnp.bfloat16)
        whitened = jnp.dot(in_inverse[position], reduced, preferred_element_type=jnp.float32).astype(jnp.bfloat16)
        carried = jnp.dot(in_carry[position], reduced, preferred_element_type=jnp.float32).astype(jnp.bfloat16)
        local_term = block_apply(whitened, out_inverse[position], False)
        middle = block_apply(carried, out_inverse[position], False).astype(jnp.bfloat16)
        results.append((local_term - pushed_prev).astype(jnp.bfloat16))
        pushed_prev = block_apply(middle, out_coupling[position], False)
    return jnp.stack(results)
```

```python
import functools

import jax
import jax.numpy as jnp
from jax import lax
from jax.experimental import pallas as pl
from jax.experimental.pallas import tpu as pltpu
from jax.sharding import PartitionSpec as P

MESH = pl.DeviceIdType.MESH
BF = jnp.bfloat16
F32 = jnp.float32


def kernel(nl, nb, nch, g_ref, s_ref, c_ref, k_ref, oi_ref, ps_ref, out_ref,
           w, gl, gn, tab, n_all, r_all, l_st, p_st, l_in, p_in,
           w_recv, w_send, w_fwd, gl_recv, gl_send, gn_recv, gn_send, t_recv, t_send,
           n_recv, n_send, r_recv, r_send, l_recv, l_send, p_recv, p_send):
    r, d = out_ref.shape
    h = d // 2
    cw = h // nch
    blk = ps_ref.shape[1]
    hb = ps_ref.shape[0] // 2
    per = cw // blk
    l = lax.axis_index("layer")
    f = lax.axis_index("feat")
    a, c = l // 2, l % 2
    b, p = f // 2, f % 2
    role = 2 * a + p
    home = c == p
    away = c != p
    chained = role < nl - 1
    core_mate = (2 * a + 1 - c, f)
    swap_mate = (l, 2 * b + 1 - p)

    def remote(src, dst, ss, rs, dev):
        return pltpu.make_async_remote_copy(
            src_ref=src, dst_ref=dst, send_sem=ss, recv_sem=rs,
            device_id=dev, device_id_type=MESH)

    def arrived(dst, sem):
        pltpu.make_async_copy(dst, dst, sem).wait()

    barrier = pltpu.get_barrier_semaphore()
    for dl in range(1, nl):
        for q in range(2):
            pl.semaphore_signal(barrier, inc=1, device_id=(lax.rem(l + dl, nl), 2 * b + q), device_id_type=MESH)
    pl.semaphore_signal(barrier, inc=1, device_id=swap_mate, device_id_type=MESH)

    @pl.when(b > 0)
    def _():
        pl.semaphore_signal(barrier, inc=1, device_id=(l, f - 2), device_id_type=MESH)

    @pl.when(b < nb - 1)
    def _():
        pl.semaphore_signal(barrier, inc=1, device_id=(l, f + 2), device_id_type=MESH)

    peers = 2 * nl - 1 + jnp.where(b > 0, 1, 0) + jnp.where(b < nb - 1, 1, 0)
    pl.semaphore_wait(barrier, peers)

    low = l + nl - 1
    low_a, low_p = (low - nl) // 2, lax.rem(low, 2)
    for hh in range(2):
        own = (l >= 1) & (c == 1) & (p == 0) & (c == hh)

        @pl.when(own)
        def _():
            pltpu.make_async_copy(g_ref.at[:, pl.ds(hh * h, h)], gn.at[p], gn_recv.at[p]).start()

        @pl.when((l >= 1) & jnp.logical_not(own))
        def _():
            remote(g_ref.at[:, pl.ds(hh * h, h)], gn.at[p], gn_send.at[hh], gn_recv.at[p],
                   (2 * low_a + hh, 2 * b + low_p)).start()

    @pl.when(home)
    def _():
        pltpu.make_async_copy(ps_ref.at[pl.ds(c * hb, hb)], tab.at[0], t_recv.at[0]).start()
        pltpu.make_async_copy(oi_ref.at[pl.ds(c * hb, hb)], tab.at[1], t_recv.at[1]).start()
        remote(ps_ref.at[pl.ds((1 - c) * hb, hb)], tab.at[0], t_send.at[0], t_recv.at[0], core_mate).start()
        remote(oi_ref.at[pl.ds((1 - c) * hb, hb)], tab.at[1], t_send.at[1], t_recv.at[1], core_mate).start()

    def g_half(hh):
        return g_ref.at[:, pl.ds(pl.multiple_of(hh * h, 128), h)]

    @pl.when(home)
    def _():
        pltpu.make_async_copy(g_half(c), gl.at[p], gl_recv.at[p]).start()
        remote(g_half(1 - c), gl.at[p], gl_send.at[0], gl_recv.at[p], core_mate).start()

    @pl.when(away)
    def _():
        remote(g_half(c), gl.at[p], gl_send.at[0], gl_recv.at[p], swap_mate).start()
        remote(g_half(1 - c), gl.at[p], gl_send.at[1], gl_recv.at[p], (2 * a + 1 - c, 2 * b + 1 - p)).start()

    weights = (c_ref, s_ref, k_ref)
    for m in range(3):
        @pl.when(home)
        def _():
            pltpu.make_async_copy(weights[m], w.at[m, p], w_recv.at[m, p]).start()
            remote(weights[m], w.at[m, p], w_send.at[m], w_recv.at[m, p], core_mate).start()

        @pl.when(away)
        def _():
            remote(weights[m], w.at[m, p], w_send.at[m], w_recv.at[m, p], swap_mate).start()

    def take_weight(m):
        arrived(w.at[m, 1 - p], w_recv.at[m, 1 - p])

        @pl.when(home)
        def _():
            remote(w.at[m, 1 - p], w.at[m, 1 - p], w_fwd.at[m], w_recv.at[m, 1 - p], core_mate).start()
        arrived(w.at[m, p], w_recv.at[m, p])

    def hop(buf, k, src, up, send, recv):
        dev = (l, f + 2) if up else (l, f - 2)
        return remote(buf.at[k, src], buf.at[k, src], send.at[k, src, 0 if up else 1], recv.at[k, src], dev)

    def pass_on(buf, send, recv, live, k, j):
        ok = live & (k >= 0) & (k < nch)
        if j == 0:
            @pl.when(ok & (b < nb - 1))
            def _():
                hop(buf, k, b, True, send, recv).start()

            @pl.when(ok & (b > 0))
            def _():
                hop(buf, k, b, False, send, recv).start()
        else:
            @pl.when(ok & (b - j >= 0))
            def _():
                arrived(buf.at[k, b - j], recv.at[k, b - j])

                @pl.when(b < nb - 1)
                def _():
                    hop(buf, k, b - j, True, send, recv).start()

            @pl.when(ok & (b + j < nb))
            def _():
                arrived(buf.at[k, b + j], recv.at[k, b + j])

                @pl.when(b > 0)
                def _():
                    hop(buf, k, b + j, False, send, recv).start()

    def sent(buf, send, recv, live, k):
        for src in range(nb):
            @pl.when(live & (src <= b) & (b < nb - 1))
            def _():
                hop(buf, k, src, True, send, recv).wait_send()

            @pl.when(live & (src >= b) & (b > 0))
            def _():
                hop(buf, k, src, False, send, recv).wait_send()

    def columns(k):
        return pl.ds(pl.multiple_of(k * cw, cw), cw)

    @pl.when(chained)
    def _():
        for q in range(2):
            arrived(gn.at[q], gn_recv.at[q])
    for i in range(2):
        arrived(tab.at[i], t_recv.at[i])

    def near_step(k):
        x = gn[:, :, columns(k)].reshape(2 * r, cw)
        parts = [lax.dot_general(x[:, i * blk:(i + 1) * blk], tab[0, k * per + i],
                                 (((1,), (1,)), ((), ())), preferred_element_type=F32).astype(BF)
                 for i in range(per)]
        n_all[k, b] = jnp.concatenate(parts, axis=1)

    def reduced_step(k):
        @pl.when(k == 0)
        def _():
            for q in range(2):
                arrived(gl.at[q], gl_recv.at[q])
            take_weight(0)

        @pl.when(chained)
        def _():
            x = n_all[k].reshape(nb * 2 * r, cw)
            coupled = jnp.dot(w[0].reshape(2 * r, d), x, preferred_element_type=F32)
            g = gl[:, :, columns(k)].reshape(2 * r, cw).astype(F32)
            r_all[k, b] = (g - coupled).astype(BF)

        @pl.when(jnp.logical_not(chained))
        def _():
            r_all[k, b] = gl[:, :, columns(k)].reshape(2 * r, cw)

    def local_copy(k, q):
        return remote(l_st.at[k, q], l_in.at[k, c], l_send.at[k, q], l_recv.at[k, c], (role, 2 * b + q))

    def push_copy(k, q):
        return remote(p_st.at[k, q], p_in.at[k, c], p_send.at[k, q], p_recv.at[k, c],
                      (lax.rem(role + 1, nl), 2 * b + q))

    def stays(q, layer):
        return (l == layer) & (p == q)

    def final_step(k):
        x = r_all[k].reshape(nb * 2 * r, cw)
        white = jnp.dot(w[1].reshape(2 * r, d), x, preferred_element_type=F32).astype(BF)
        for i in range(per):
            o = jnp.dot(white[:, i * blk:(i + 1) * blk], tab[1, k * per + i], preferred_element_type=F32)
            l_st[k, :, :, i * blk:(i + 1) * blk] = o.astype(BF).reshape(2, r, blk)
        for q in range(2):
            @pl.when(stays(q, role))
            def _():
                pltpu.make_async_copy(l_st.at[k, q], l_in.at[k, c], l_recv.at[k, c]).start()

            @pl.when(jnp.logical_not(stays(q, role)))
            def _():
                local_copy(k, q).start()

        @pl.when(chained)
        def _():
            y = r_all[k].reshape(nb * 2 * r, cw)
            carried = jnp.dot(w[2].reshape(2 * r, d), y, preferred_element_type=F32).astype(BF)
            for i in range(per):
                mid = jnp.dot(carried[:, i * blk:(i + 1) * blk], tab[1, k * per + i],
                              preferred_element_type=F32).astype(BF)
                o = jnp.dot(mid, tab[0, k * per + i], preferred_element_type=F32)
                p_st[k, :, :, i * blk:(i + 1) * blk] = o.astype(BF).reshape(2, r, blk)
            for q in range(2):
                @pl.when(stays(q, role + 1))
                def _():
                    pltpu.make_async_copy(p_st.at[k, q], p_in.at[k, c], p_recv.at[k, c]).start()

                @pl.when(jnp.logical_not(stays(q, role + 1)))
                def _():
                    push_copy(k, q).start()

    def out_step(k):
        for hh in range(2):
            arrived(l_in.at[k, hh], l_recv.at[k, hh])
            dst = pl.ds(pl.multiple_of(hh * h + k * cw, cw), cw)

            @pl.when(l > 0)
            def _():
                arrived(p_in.at[k, hh], p_recv.at[k, hh])
                out_ref[:, dst] = (l_in[k, hh].astype(F32) - p_in[k, hh].astype(F32)).astype(BF)

            @pl.when(l == 0)
            def _():
                out_ref[:, dst] = l_in[k, hh]

    def inside(k):
        return (k >= 0) & (k < nch)

    n_lag = nb - 1
    r_lag = 2 * (nb - 1)

    def step(t, carry):
        @pl.when(chained & inside(t))
        def _():
            near_step(t)
        for j in range(nb):
            pass_on(n_all, n_send, n_recv, chained, t - j, j)
        kr = t - n_lag

        @pl.when(inside(kr))
        def _():
            reduced_step(kr)
        for j in range(nb):
            pass_on(r_all, r_send, r_recv, True, kr - j, j)

        @pl.when(kr == min(1, nch - 1))
        def _():
            take_weight(1)

        @pl.when(kr == min(2, nch - 1))
        def _():
            take_weight(2)
        kf = t - r_lag

        @pl.when(inside(kf))
        def _():
            final_step(kf)
        ko = kf - 1

        @pl.when(inside(ko))
        def _():
            out_step(ko)
        return carry

    lax.fori_loop(0, nch + r_lag + 1, step, 0)

    def drain(k, carry):
        sent(n_all, n_send, n_recv, chained, k)
        sent(r_all, r_send, r_recv, True, k)
        for q in range(2):
            @pl.when(jnp.logical_not(stays(q, role)))
            def _():
                local_copy(k, q).wait_send()

            @pl.when(chained & jnp.logical_not(stays(q, role + 1)))
            def _():
                push_copy(k, q).wait_send()
        return carry

    lax.fori_loop(0, nch, drain, 0)

    for hh in range(2):
        own = (l >= 1) & (c == 1) & (p == 0) & (c == hh)

        @pl.when((l >= 1) & jnp.logical_not(own))
        def _():
            remote(g_ref.at[:, pl.ds(hh * h, h)], gn.at[p], gn_send.at[hh], gn_recv.at[p],
                   (2 * low_a + hh, 2 * b + low_p)).wait_send()

    @pl.when(home)
    def _():
        for i, src in enumerate((ps_ref, oi_ref)):
            remote(src.at[pl.ds((1 - c) * hb, hb)], tab.at[i], t_send.at[i], t_recv.at[i], core_mate).wait_send()
        remote(g_half(1 - c), gl.at[p], gl_send.at[0], gl_recv.at[p], core_mate).wait_send()
        for m in range(3):
            remote(w.at[m, 1 - p], w.at[m, 1 - p], w_fwd.at[m], w_recv.at[m, 1 - p], core_mate).wait_send()

    @pl.when(away)
    def _():
        remote(g_half(c), gl.at[p], gl_send.at[0], gl_recv.at[p], swap_mate).wait_send()
        remote(g_half(1 - c), gl.at[p], gl_send.at[1], gl_recv.at[p], swap_mate).wait_send()
    for m in range(3):
        remote(weights[m], w.at[m, p], w_send.at[m], w_recv.at[m, p], core_mate).wait_send()


def local(nl, nf, gradient, in_inverse, in_coupling, in_carry, out_inverse, out_coupling):
    g = gradient[0]
    r, d = g.shape
    nb = nf // 2
    blocks, blk = out_inverse.shape[1], out_inverse.shape[2]
    h = d // 2
    hb = blocks // 2
    nch = hb // 2 if hb % 2 == 0 else hb
    cw = h // nch
    dma = pltpu.SemaphoreType.DMA
    vm = pltpu.VMEM
    anyspec = pl.BlockSpec(memory_space=pl.ANY)
    out = pl.pallas_call(
        functools.partial(kernel, nl, nb, nch),
        out_shape=jax.ShapeDtypeStruct((r, d), BF),
        in_specs=[anyspec] * 6,
        out_specs=pl.BlockSpec(memory_space=pltpu.VMEM),
        scratch_shapes=[
            vm((3, 2, r, d), BF), vm((2, r, h), BF), vm((2, r, h), BF), vm((2, hb, blk, blk), BF),
            vm((nch, nb, 2 * r, cw), BF), vm((nch, nb, 2 * r, cw), BF),
            vm((nch, 2, r, cw), BF), vm((nch, 2, r, cw), BF), vm((nch, 2, r, cw), BF), vm((nch, 2, r, cw), BF),
            dma((3, 2)), dma((3,)), dma((3,)), dma((2,)), dma((2,)), dma((2,)), dma((2,)), dma((2,)), dma((2,)),
            dma((nch, nb)), dma((nch, nb, 2)), dma((nch, nb)), dma((nch, nb, 2)),
            dma((nch, 2)), dma((nch, 2)), dma((nch, 2)), dma((nch, 2)),
        ],
        compiler_params=pltpu.CompilerParams(
            collective_id=0, has_side_effects=True, vmem_limit_bytes=62 * 1024 * 1024),
    )(g, in_inverse[0], in_coupling[0], in_carry[0], out_inverse[0], out_coupling[0])
    return out[None]


def solution(mesh):
    return jax.shard_map(
        functools.partial(local, mesh.shape["layer"], mesh.shape["feat"]),
        mesh=mesh,
        in_specs=(
            P("layer", "feat", None),
            P("layer", "feat", None),
            P("layer", "feat", None),
            P("layer", "feat", None),
            P("layer", None, None, None),
            P("layer", None, None, None),
        ),
        out_specs=P("layer", "feat", None),
        check_vma=False,
    )
```

```python
import functools

import jax
import jax.numpy as jnp
from jax import lax
from jax.experimental import pallas as pl
from jax.experimental.pallas import tpu as pltpu
from jax.sharding import PartitionSpec as P

MESH = pl.DeviceIdType.MESH
BF = jnp.bfloat16
F32 = jnp.float32


def kernel(nl, nb, nch, g_ref, s_ref, c_ref, k_ref, oi_ref, ps_ref, out_ref,
           w, gl, gn, tab, n_all, r_all, l_st, p_st, l_in, p_in,
           w_recv, w_send, w_fwd, gl_recv, gl_send, gn_recv, gn_send, t_recv, t_send,
           n_recv, n_send, r_recv, r_send, l_recv, l_send, p_recv, p_send):
    r, d = out_ref.shape
    h = d // 2
    cw = h // nch
    blk = ps_ref.shape[1]
    hb = ps_ref.shape[0] // 2
    per = cw // blk
    l = lax.axis_index("layer")
    f = lax.axis_index("feat")
    a, c = l // 2, l % 2
    b, p = f // 2, f % 2
    role = 2 * a + p
    home = c == p
    away = c != p
    chained = role < nl - 1
    core_mate = (2 * a + 1 - c, f)
    swap_mate = (l, 2 * b + 1 - p)

    def remote(src, dst, ss, rs, dev):
        return pltpu.make_async_remote_copy(
            src_ref=src, dst_ref=dst, send_sem=ss, recv_sem=rs,
            device_id=dev, device_id_type=MESH)

    def arrived(dst, sem):
        pltpu.make_async_copy(dst, dst, sem).wait()

    barrier = pltpu.get_barrier_semaphore()
    for dl in range(1, nl):
        for q in range(2):
            pl.semaphore_signal(barrier, inc=1, device_id=(lax.rem(l + dl, nl), 2 * b + q), device_id_type=MESH)
    pl.semaphore_signal(barrier, inc=1, device_id=swap_mate, device_id_type=MESH)

    @pl.when(b > 0)
    def _():
        pl.semaphore_signal(barrier, inc=1, device_id=(l, f - 2), device_id_type=MESH)

    @pl.when(b < nb - 1)
    def _():
        pl.semaphore_signal(barrier, inc=1, device_id=(l, f + 2), device_id_type=MESH)

    peers = 2 * nl - 1 + jnp.where(b > 0, 1, 0) + jnp.where(b < nb - 1, 1, 0)
    pl.semaphore_wait(barrier, peers)

    low = l + nl - 1
    low_a, low_p = (low - nl) // 2, lax.rem(low, 2)

    def above_cols(hh, k):
        return g_ref.at[:, pl.ds(pl.multiple_of(hh * h + k * cw, cw), cw)]

    def above_stays(hh):
        return (l >= 1) & (c == 1) & (p == 0) & (c == hh)

    def above_copy(hh, k):
        return remote(above_cols(hh, k), gn.at[k, p], gn_send.at[k, hh], gn_recv.at[k, p],
                      (2 * low_a + hh, 2 * b + low_p))

    def send_above(k, carry):
        for hh in range(2):
            @pl.when(above_stays(hh))
            def _():
                pltpu.make_async_copy(above_cols(hh, k), gn.at[k, p], gn_recv.at[k, p]).start()

            @pl.when((l >= 1) & jnp.logical_not(above_stays(hh)))
            def _():
                above_copy(hh, k).start()
        return carry

    lax.fori_loop(0, nch, send_above, 0)

    @pl.when(home)
    def _():
        pltpu.make_async_copy(ps_ref.at[pl.ds(c * hb, hb)], tab.at[0], t_recv.at[0]).start()
        pltpu.make_async_copy(oi_ref.at[pl.ds(c * hb, hb)], tab.at[1], t_recv.at[1]).start()
        remote(ps_ref.at[pl.ds((1 - c) * hb, hb)], tab.at[0], t_send.at[0], t_recv.at[0], core_mate).start()
        remote(oi_ref.at[pl.ds((1 - c) * hb, hb)], tab.at[1], t_send.at[1], t_recv.at[1], core_mate).start()

    def g_half(hh):
        return g_ref.at[:, pl.ds(pl.multiple_of(hh * h, 128), h)]

    @pl.when(home)
    def _():
        pltpu.make_async_copy(g_half(c), gl.at[p], gl_recv.at[p]).start()
        remote(g_half(1 - c), gl.at[p], gl_send.at[0], gl_recv.at[p], core_mate).start()

    @pl.when(away)
    def _():
        remote(g_half(c), gl.at[p], gl_send.at[0], gl_recv.at[p], swap_mate).start()
        remote(g_half(1 - c), gl.at[p], gl_send.at[1], gl_recv.at[p], (2 * a + 1 - c, 2 * b + 1 - p)).start()

    weights = (c_ref, s_ref, k_ref)
    for m in range(3):
        @pl.when(home)
        def _():
            pltpu.make_async_copy(weights[m], w.at[m, p], w_recv.at[m, p]).start()
            remote(weights[m], w.at[m, p], w_send.at[m], w_recv.at[m, p], core_mate).start()

        @pl.when(away)
        def _():
            remote(weights[m], w.at[m, p], w_send.at[m], w_recv.at[m, p], swap_mate).start()

    def take_weight(m):
        arrived(w.at[m, 1 - p], w_recv.at[m, 1 - p])

        @pl.when(home)
        def _():
            remote(w.at[m, 1 - p], w.at[m, 1 - p], w_fwd.at[m], w_recv.at[m, 1 - p], core_mate).start()
        arrived(w.at[m, p], w_recv.at[m, p])

    def hop(buf, k, src, up, send, recv):
        dev = (l, f + 2) if up else (l, f - 2)
        return remote(buf.at[k, src], buf.at[k, src], send.at[k, src, 0 if up else 1], recv.at[k, src], dev)

    def pass_on(buf, send, recv, live, k, j):
        ok = live & (k >= 0) & (k < nch)
        if j == 0:
            @pl.when(ok & (b < nb - 1))
            def _():
                hop(buf, k, b, True, send, recv).start()

            @pl.when(ok & (b > 0))
            def _():
                hop(buf, k, b, False, send, recv).start()
        else:
            @pl.when(ok & (b - j >= 0))
            def _():
                arrived(buf.at[k, b - j], recv.at[k, b - j])

                @pl.when(b < nb - 1)
                def _():
                    hop(buf, k, b - j, True, send, recv).start()

            @pl.when(ok & (b + j < nb))
            def _():
                arrived(buf.at[k, b + j], recv.at[k, b + j])

                @pl.when(b > 0)
                def _():
                    hop(buf, k, b + j, False, send, recv).start()

    def sent(buf, send, recv, live, k):
        for src in range(nb):
            @pl.when(live & (src <= b) & (b < nb - 1))
            def _():
                hop(buf, k, src, True, send, recv).wait_send()

            @pl.when(live & (src >= b) & (b > 0))
            def _():
                hop(buf, k, src, False, send, recv).wait_send()

    def columns(k):
        return pl.ds(pl.multiple_of(k * cw, cw), cw)

    for i in range(2):
        arrived(tab.at[i], t_recv.at[i])

    def near_step(k):
        for q in range(2):
            arrived(gn.at[k, q], gn_recv.at[k, q])
        x = gn[k].reshape(2 * r, cw)
        parts = [lax.dot_general(x[:, i * blk:(i + 1) * blk], tab[0, k * per + i],
                                 (((1,), (1,)), ((), ())), preferred_element_type=F32).astype(BF)
                 for i in range(per)]
        n_all[k, b] = jnp.concatenate(parts, axis=1)

    def reduced_step(k):
        @pl.when(k == 0)
        def _():
            for q in range(2):
                arrived(gl.at[q], gl_recv.at[q])
            take_weight(0)

        @pl.when(chained)
        def _():
            x = n_all[k].reshape(nb * 2 * r, cw)
            coupled = jnp.dot(w[0].reshape(2 * r, d), x, preferred_element_type=F32)
            g = gl[:, :, columns(k)].reshape(2 * r, cw).astype(F32)
            r_all[k, b] = (g - coupled).astype(BF)

        @pl.when(jnp.logical_not(chained))
        def _():
            r_all[k, b] = gl[:, :, columns(k)].reshape(2 * r, cw)

    def local_copy(k, q):
        return remote(l_st.at[k, q], l_in.at[k, c], l_send.at[k, q], l_recv.at[k, c], (role, 2 * b + q))

    def push_copy(k, q):
        return remote(p_st.at[k, q], p_in.at[k, c], p_send.at[k, q], p_recv.at[k, c],
                      (lax.rem(role + 1, nl), 2 * b + q))

    def stays(q, layer):
        return (l == layer) & (p == q)

    def final_step(k):
        x = r_all[k].reshape(nb * 2 * r, cw)
        white = jnp.dot(w[1].reshape(2 * r, d), x, preferred_element_type=F32).astype(BF)
        for i in range(per):
            o = jnp.dot(white[:, i * blk:(i + 1) * blk], tab[1, k * per + i], preferred_element_type=F32)
            l_st[k, :, :, i * blk:(i + 1) * blk] = o.astype(BF).reshape(2, r, blk)
        for q in range(2):
            @pl.when(stays(q, role))
            def _():
                pltpu.make_async_copy(l_st.at[k, q], l_in.at[k, c], l_recv.at[k, c]).start()

            @pl.when(jnp.logical_not(stays(q, role)))
            def _():
                local_copy(k, q).start()

        @pl.when(chained)
        def _():
            y = r_all[k].reshape(nb * 2 * r, cw)
            carried = jnp.dot(w[2].reshape(2 * r, d), y, preferred_element_type=F32).astype(BF)
            for i in range(per):
                mid = jnp.dot(carried[:, i * blk:(i + 1) * blk], tab[1, k * per + i],
                              preferred_element_type=F32).astype(BF)
                o = jnp.dot(mid, tab[0, k * per + i], preferred_element_type=F32)
                p_st[k, :, :, i * blk:(i + 1) * blk] = o.astype(BF).reshape(2, r, blk)
            for q in range(2):
                @pl.when(stays(q, role + 1))
                def _():
                    pltpu.make_async_copy(p_st.at[k, q], p_in.at[k, c], p_recv.at[k, c]).start()

                @pl.when(jnp.logical_not(stays(q, role + 1)))
                def _():
                    push_copy(k, q).start()

    def out_step(k):
        for hh in range(2):
            arrived(l_in.at[k, hh], l_recv.at[k, hh])
            dst = pl.ds(pl.multiple_of(hh * h + k * cw, cw), cw)

            @pl.when(l > 0)
            def _():
                arrived(p_in.at[k, hh], p_recv.at[k, hh])
                out_ref[:, dst] = (l_in[k, hh].astype(F32) - p_in[k, hh].astype(F32)).astype(BF)

            @pl.when(l == 0)
            def _():
                out_ref[:, dst] = l_in[k, hh]

    def inside(k):
        return (k >= 0) & (k < nch)

    n_lag = nb - 1
    r_lag = 2 * (nb - 1)

    def step(t, carry):
        @pl.when(chained & inside(t))
        def _():
            near_step(t)
        for j in range(nb):
            pass_on(n_all, n_send, n_recv, chained, t - j, j)
        kr = t - n_lag

        @pl.when(inside(kr))
        def _():
            reduced_step(kr)
        for j in range(nb):
            pass_on(r_all, r_send, r_recv, True, kr - j, j)

        @pl.when(kr == min(1, nch - 1))
        def _():
            take_weight(1)

        @pl.when(kr == min(2, nch - 1))
        def _():
            take_weight(2)
        kf = t - r_lag

        @pl.when(inside(kf))
        def _():
            final_step(kf)
        ko = kf - 1

        @pl.when(inside(ko))
        def _():
            out_step(ko)
        return carry

    lax.fori_loop(0, nch + r_lag + 1, step, 0)

    def drain(k, carry):
        sent(n_all, n_send, n_recv, chained, k)
        sent(r_all, r_send, r_recv, True, k)
        for q in range(2):
            @pl.when((l >= 1) & jnp.logical_not(above_stays(q)))
            def _():
                above_copy(q, k).wait_send()

            @pl.when(jnp.logical_not(stays(q, role)))
            def _():
                local_copy(k, q).wait_send()

            @pl.when(chained & jnp.logical_not(stays(q, role + 1)))
            def _():
                push_copy(k, q).wait_send()
        return carry

    lax.fori_loop(0, nch, drain, 0)

    @pl.when(home)
    def _():
        for i, src in enumerate((ps_ref, oi_ref)):
            remote(src.at[pl.ds((1 - c) * hb, hb)], tab.at[i], t_send.at[i], t_recv.at[i], core_mate).wait_send()
        remote(g_half(1 - c), gl.at[p], gl_send.at[0], gl_recv.at[p], core_mate).wait_send()
        for m in range(3):
            remote(w.at[m, 1 - p], w.at[m, 1 - p], w_fwd.at[m], w_recv.at[m, 1 - p], core_mate).wait_send()

    @pl.when(away)
    def _():
        remote(g_half(c), gl.at[p], gl_send.at[0], gl_recv.at[p], swap_mate).wait_send()
        remote(g_half(1 - c), gl.at[p], gl_send.at[1], gl_recv.at[p], swap_mate).wait_send()
    for m in range(3):
        remote(weights[m], w.at[m, p], w_send.at[m], w_recv.at[m, p], core_mate).wait_send()


def local(nl, nf, gradient, in_inverse, in_coupling, in_carry, out_inverse, out_coupling):
    g = gradient[0]
    r, d = g.shape
    nb = nf // 2
    blocks, blk = out_inverse.shape[1], out_inverse.shape[2]
    h = d // 2
    hb = blocks // 2
    nch = hb // 2 if hb % 2 == 0 else hb
    cw = h // nch
    dma = pltpu.SemaphoreType.DMA
    vm = pltpu.VMEM
    anyspec = pl.BlockSpec(memory_space=pl.ANY)
    out = pl.pallas_call(
        functools.partial(kernel, nl, nb, nch),
        out_shape=jax.ShapeDtypeStruct((r, d), BF),
        in_specs=[anyspec] * 6,
        out_specs=pl.BlockSpec(memory_space=pltpu.VMEM),
        scratch_shapes=[
            vm((3, 2, r, d), BF), vm((2, r, h), BF), vm((nch, 2, r, cw), BF), vm((2, hb, blk, blk), BF),
            vm((nch, nb, 2 * r, cw), BF), vm((nch, nb, 2 * r, cw), BF),
            vm((nch, 2, r, cw), BF), vm((nch, 2, r, cw), BF), vm((nch, 2, r, cw), BF), vm((nch, 2, r, cw), BF),
            dma((3, 2)), dma((3,)), dma((3,)), dma((2,)), dma((2,)), dma((nch, 2)), dma((nch, 2)), dma((2,)), dma((2,)),
            dma((nch, nb)), dma((nch, nb, 2)), dma((nch, nb)), dma((nch, nb, 2)),
            dma((nch, 2)), dma((nch, 2)), dma((nch, 2)), dma((nch, 2)),
        ],
        compiler_params=pltpu.CompilerParams(
            collective_id=0, has_side_effects=True, vmem_limit_bytes=62 * 1024 * 1024),
    )(g, in_inverse[0], in_coupling[0], in_carry[0], out_inverse[0], out_coupling[0])
    return out[None]


def solution(mesh):
    return jax.shard_map(
        functools.partial(local, mesh.shape["layer"], mesh.shape["feat"]),
        mesh=mesh,
        in_specs=(
            P("layer", "feat", None),
            P("layer", "feat", None),
            P("layer", "feat", None),
            P("layer", "feat", None),
            P("layer", None, None, None),
            P("layer", None, None, None),
        ),
        out_specs=P("layer", "feat", None),
        check_vma=False,
    )
```

```python
import functools

import jax
import jax.numpy as jnp
from jax import lax
from jax.experimental import pallas as pl
from jax.experimental.pallas import tpu as pltpu
from jax.sharding import PartitionSpec as P

MESH = pl.DeviceIdType.MESH
BF = jnp.bfloat16
F32 = jnp.float32


def kernel(nl, nb, nch, lent, g_ref, s_ref, c_ref, k_ref, oi_ref, ps_ref, out_ref,
           w, gl, gn, tab, n_all, r_all, l_st, p_st, l_in, p_in, w2, gl2, gn2, l_st2, p_st2,
           w_recv, w_send, w_fwd, gl_recv, gl_send, gn_recv, gn_send, t_recv, t_send,
           n_recv, n_send, r_recv, r_send, l_recv, l_send, p_recv, p_send,
           w2_recv, w2_send, w2_fwd, gl2_recv, gl2_send, gn2_recv, gn2_send, l2_send, p2_send):
    r, d = out_ref.shape
    h = d // 2
    cw = h // nch
    blk = ps_ref.shape[1]
    hb = ps_ref.shape[0] // 2
    per = cw // blk
    l = lax.axis_index("layer")
    f = lax.axis_index("feat")
    a, c = l // 2, l % 2
    b, p = f // 2, f % 2
    role = 2 * a + p
    home = c == p
    away = c != p
    chained = role < nl - 1
    core_mate = (2 * a + 1 - c, f)
    swap_mate = (l, 2 * b + 1 - p)

    def remote(src, dst, ss, rs, dev):
        return pltpu.make_async_remote_copy(
            src_ref=src, dst_ref=dst, send_sem=ss, recv_sem=rs,
            device_id=dev, device_id_type=MESH)

    def arrived(dst, sem):
        pltpu.make_async_copy(dst, dst, sem).wait()

    barrier = pltpu.get_barrier_semaphore()
    for dl in range(1, nl):
        for q in range(2):
            pl.semaphore_signal(barrier, inc=1, device_id=(lax.rem(l + dl, nl), 2 * b + q), device_id_type=MESH)
    pl.semaphore_signal(barrier, inc=1, device_id=swap_mate, device_id_type=MESH)

    first_lent = nch - lent
    is_end = (b == 0) | (b == nb - 1)
    helps = (b == 1) | (b == nb - 2)
    mate_b = jnp.where((b == 0) | (b == nb - 1), jnp.where(b == 0, 1, nb - 2), jnp.where(b == 1, 0, nb - 1))
    if not lent:
        is_end = helps = b < 0
    paired = is_end | helps

    def mate(layer, q):
        return (layer, 2 * mate_b + q)

    @pl.when(paired)
    def _():
        for dl in range(nl):
            for q in range(2):
                pl.semaphore_signal(barrier, inc=1, device_id=mate(dl, q), device_id_type=MESH)

    low_plain = (b > 0) & jnp.logical_not(paired & (mate_b == b - 1))
    high_plain = (b < nb - 1) & jnp.logical_not(paired & (mate_b == b + 1))

    @pl.when(low_plain)
    def _():
        pl.semaphore_signal(barrier, inc=1, device_id=(l, f - 2), device_id_type=MESH)

    @pl.when(high_plain)
    def _():
        pl.semaphore_signal(barrier, inc=1, device_id=(l, f + 2), device_id_type=MESH)

    peers = 2 * nl - 1 + jnp.where(paired, 2 * nl, 0) + jnp.where(low_plain, 1, 0) + jnp.where(high_plain, 1, 0)
    pl.semaphore_wait(barrier, peers)

    low = l + nl - 1
    low_a, low_p = (low - nl) // 2, lax.rem(low, 2)

    def above_cols(hh, k):
        return g_ref.at[:, pl.ds(pl.multiple_of(hh * h + k * cw, cw), cw)]

    def above_stays(hh):
        return (l >= 1) & (c == 1) & (p == 0) & (c == hh)

    def above_copy(hh, k):
        return remote(above_cols(hh, k), gn.at[k, p], gn_send.at[k, hh], gn_recv.at[k, p],
                      (2 * low_a + hh, 2 * b + low_p))

    def send_above(k, carry):
        for hh in range(2):
            @pl.when(above_stays(hh))
            def _():
                pltpu.make_async_copy(above_cols(hh, k), gn.at[k, p], gn_recv.at[k, p]).start()

            @pl.when((l >= 1) & jnp.logical_not(above_stays(hh)))
            def _():
                above_copy(hh, k).start()
        return carry

    lax.fori_loop(0, nch, send_above, 0)

    @pl.when(home)
    def _():
        pltpu.make_async_copy(ps_ref.at[pl.ds(c * hb, hb)], tab.at[0], t_recv.at[0]).start()
        pltpu.make_async_copy(oi_ref.at[pl.ds(c * hb, hb)], tab.at[1], t_recv.at[1]).start()
        remote(ps_ref.at[pl.ds((1 - c) * hb, hb)], tab.at[0], t_send.at[0], t_recv.at[0], core_mate).start()
        remote(oi_ref.at[pl.ds((1 - c) * hb, hb)], tab.at[1], t_send.at[1], t_recv.at[1], core_mate).start()

    def g_half(hh):
        return g_ref.at[:, pl.ds(pl.multiple_of(hh * h, 128), h)]

    @pl.when(home)
    def _():
        pltpu.make_async_copy(g_half(c), gl.at[p], gl_recv.at[p]).start()
        remote(g_half(1 - c), gl.at[p], gl_send.at[0], gl_recv.at[p], core_mate).start()

    @pl.when(away)
    def _():
        remote(g_half(c), gl.at[p], gl_send.at[0], gl_recv.at[p], swap_mate).start()
        remote(g_half(1 - c), gl.at[p], gl_send.at[1], gl_recv.at[p], (2 * a + 1 - c, 2 * b + 1 - p)).start()

    weights = (c_ref, s_ref, k_ref)
    for m in range(3):
        @pl.when(home)
        def _():
            pltpu.make_async_copy(weights[m], w.at[m, p], w_recv.at[m, p]).start()
            remote(weights[m], w.at[m, p], w_send.at[m], w_recv.at[m, p], core_mate).start()

        @pl.when(away)
        def _():
            remote(weights[m], w.at[m, p], w_send.at[m], w_recv.at[m, p], swap_mate).start()

    def take_weight(m):
        arrived(w.at[m, 1 - p], w_recv.at[m, 1 - p])

        @pl.when(home)
        def _():
            remote(w.at[m, 1 - p], w.at[m, 1 - p], w_fwd.at[m], w_recv.at[m, 1 - p], core_mate).start()
        waited = home & is_end

        @pl.when(jnp.logical_not(waited))
        def _():
            arrived(w.at[m, p], w_recv.at[m, p])

    def hop(buf, k, src, up, send, recv):
        dev = (l, f + 2) if up else (l, f - 2)
        return remote(buf.at[k, src], buf.at[k, src], send.at[k, src, 0 if up else 1], recv.at[k, src], dev)

    def is_lent(k):
        return k >= first_lent

    def takes_part(k):
        return jnp.logical_not(is_lent(k) & is_end)

    def goes_up(k):
        return (b < nb - 1) & takes_part(k) & jnp.logical_not(is_lent(k) & (b + 1 == nb - 1))

    def goes_down(k):
        return (b > 0) & takes_part(k) & jnp.logical_not(is_lent(k) & (b - 1 == 0))

    def made_here(k, src):
        return is_lent(k) & helps & (src == mate_b)

    def pass_on(buf, send, recv, live, k, j):
        ok = live & (k >= 0) & (k < nch) & takes_part(k)
        if j == 0:
            @pl.when(ok & goes_up(k))
            def _():
                hop(buf, k, b, True, send, recv).start()

            @pl.when(ok & goes_down(k))
            def _():
                hop(buf, k, b, False, send, recv).start()
        else:
            for src, there, onward, up in ((b - j, b - j >= 0, goes_up(k), True),
                                           (b + j, b + j < nb, goes_down(k), False)):
                @pl.when(ok & there & jnp.logical_not(made_here(k, src)))
                def _():
                    arrived(buf.at[k, src], recv.at[k, src])

                @pl.when(ok & there & onward)
                def _():
                    hop(buf, k, src, up, send, recv).start()

    def sent(buf, send, recv, live, k):
        for src in range(nb):
            @pl.when(live & (src <= b) & goes_up(k))
            def _():
                hop(buf, k, src, True, send, recv).wait_send()

            @pl.when(live & (src >= b) & goes_down(k))
            def _():
                hop(buf, k, src, False, send, recv).wait_send()

    def columns(k):
        return pl.ds(pl.multiple_of(k * cw, cw), cw)

    for i in range(2):
        arrived(tab.at[i], t_recv.at[i])

    def near_of(x, k):
        parts = [lax.dot_general(x[:, i * blk:(i + 1) * blk], tab[0, k * per + i],
                                 (((1,), (1,)), ((), ())), preferred_element_type=F32).astype(BF)
                 for i in range(per)]
        return jnp.concatenate(parts, axis=1)

    def lend_above(k):
        return remote(gn.at[k], gn2.at[k - first_lent], gn2_send.at[k - first_lent],
                      gn2_recv.at[k - first_lent], mate(l, p))

    def lend_own():
        cols = pl.ds(first_lent * cw, lent * cw)
        return remote(gl.at[:, :, cols], gl2, gl2_send, gl2_recv, mate(l, p))

    def lend_weight(m, q):
        return remote(w.at[m, q], w2.at[m, q], w2_send.at[m, q], w2_recv.at[m, q], mate(l, p))

    def share_weight(m, q):
        return remote(w2.at[m, q], w2.at[m, q], w2_fwd.at[m, q], w2_recv.at[m, q], core_mate)

    def take_lent(m):
        for q in range(2):
            arrived(w2.at[m, q], w2_recv.at[m, q])

            @pl.when(home)
            def _():
                share_weight(m, q).start()

    def near_step(k):
        for q in range(2):
            arrived(gn.at[k, q], gn_recv.at[k, q])

        @pl.when(takes_part(k))
        def _():
            n_all[k, b] = near_of(gn[k].reshape(2 * r, cw), k)

        if lent:
            @pl.when(jnp.logical_not(takes_part(k)))
            def _():
                lend_above(k).start()

    def near_lent(k):
        i = k - first_lent
        arrived(gn2.at[i], gn2_recv.at[i])
        n_all[k, mate_b] = near_of(gn2[i].reshape(2 * r, cw), k)

    def reduced_lent(k):
        cols = pl.ds(pl.multiple_of((k - first_lent) * cw, cw), cw)

        @pl.when(k == first_lent)
        def _():
            arrived(gl2, gl2_recv)

        @pl.when(chained)
        def _():
            x = n_all[k].reshape(nb * 2 * r, cw)
            coupled = jnp.dot(w2[0].reshape(2 * r, d), x, preferred_element_type=F32)
            r_all[k, mate_b] = (gl2[:, :, cols].reshape(2 * r, cw).astype(F32) - coupled).astype(BF)

        @pl.when(jnp.logical_not(chained))
        def _():
            r_all[k, mate_b] = gl2[:, :, cols].reshape(2 * r, cw)

    def local_lent(k, q):
        i = k - first_lent
        return remote(l_st2.at[i, q], l_in.at[k, c], l2_send.at[i, q], l_recv.at[k, c], mate(role, q))

    def push_lent(k, q):
        i = k - first_lent
        return remote(p_st2.at[i, q], p_in.at[k, c], p2_send.at[i, q], p_recv.at[k, c],
                      mate(lax.rem(role + 1, nl), q))

    def final_lent(k):
        i = k - first_lent
        x = r_all[k].reshape(nb * 2 * r, cw)
        white = jnp.dot(w2[1].reshape(2 * r, d), x, preferred_element_type=F32).astype(BF)
        for n in range(per):
            o = jnp.dot(white[:, n * blk:(n + 1) * blk], tab[1, k * per + n], preferred_element_type=F32)
            l_st2[i, :, :, n * blk:(n + 1) * blk] = o.astype(BF).reshape(2, r, blk)
        for q in range(2):
            local_lent(k, q).start()

        @pl.when(chained)
        def _():
            y = r_all[k].reshape(nb * 2 * r, cw)
            carried = jnp.dot(w2[2].reshape(2 * r, d), y, preferred_element_type=F32).astype(BF)
            for n in range(per):
                mid = jnp.dot(carried[:, n * blk:(n + 1) * blk], tab[1, k * per + n],
                              preferred_element_type=F32).astype(BF)
                o = jnp.dot(mid, tab[0, k * per + n], preferred_element_type=F32)
                p_st2[i, :, :, n * blk:(n + 1) * blk] = o.astype(BF).reshape(2, r, blk)
            for q in range(2):
                push_lent(k, q).start()

    def reduced_step(k):
        @pl.when(chained)
        def _():
            x = n_all[k].reshape(nb * 2 * r, cw)
            coupled = jnp.dot(w[0].reshape(2 * r, d), x, preferred_element_type=F32)
            g = gl[:, :, columns(k)].reshape(2 * r, cw).astype(F32)
            r_all[k, b] = (g - coupled).astype(BF)

        @pl.when(jnp.logical_not(chained))
        def _():
            r_all[k, b] = gl[:, :, columns(k)].reshape(2 * r, cw)

    def local_copy(k, q):
        return remote(l_st.at[k, q], l_in.at[k, c], l_send.at[k, q], l_recv.at[k, c], (role, 2 * b + q))

    def push_copy(k, q):
        return remote(p_st.at[k, q], p_in.at[k, c], p_send.at[k, q], p_recv.at[k, c],
                      (lax.rem(role + 1, nl), 2 * b + q))

    def stays(q, layer):
        return (l == layer) & (p == q)

    def final_step(k):
        x = r_all[k].reshape(nb * 2 * r, cw)
        white = jnp.dot(w[1].reshape(2 * r, d), x, preferred_element_type=F32).astype(BF)
        for i in range(per):
            o = jnp.dot(white[:, i * blk:(i + 1) * blk], tab[1, k * per + i], preferred_element_type=F32)
            l_st[k, :, :, i * blk:(i + 1) * blk] = o.astype(BF).reshape(2, r, blk)
        for q in range(2):
            @pl.when(stays(q, role))
            def _():
                pltpu.make_async_copy(l_st.at[k, q], l_in.at[k, c], l_recv.at[k, c]).start()

            @pl.when(jnp.logical_not(stays(q, role)))
            def _():
                local_copy(k, q).start()

        @pl.when(chained)
        def _():
            y = r_all[k].reshape(nb * 2 * r, cw)
            carried = jnp.dot(w[2].reshape(2 * r, d), y, preferred_element_type=F32).astype(BF)
            for i in range(per):
                mid = jnp.dot(carried[:, i * blk:(i + 1) * blk], tab[1, k * per + i],
                              preferred_element_type=F32).astype(BF)
                o = jnp.dot(mid, tab[0, k * per + i], preferred_element_type=F32)
                p_st[k, :, :, i * blk:(i + 1) * blk] = o.astype(BF).reshape(2, r, blk)
            for q in range(2):
                @pl.when(stays(q, role + 1))
                def _():
                    pltpu.make_async_copy(p_st.at[k, q], p_in.at[k, c], p_recv.at[k, c]).start()

                @pl.when(jnp.logical_not(stays(q, role + 1)))
                def _():
                    push_copy(k, q).start()

    def out_step(k):
        for hh in range(2):
            arrived(l_in.at[k, hh], l_recv.at[k, hh])
            dst = pl.ds(pl.multiple_of(hh * h + k * cw, cw), cw)

            @pl.when(l > 0)
            def _():
                arrived(p_in.at[k, hh], p_recv.at[k, hh])
                out_ref[:, dst] = (l_in[k, hh].astype(F32) - p_in[k, hh].astype(F32)).astype(BF)

            @pl.when(l == 0)
            def _():
                out_ref[:, dst] = l_in[k, hh]

    def inside(k):
        return (k >= 0) & (k < nch)

    n_lag = nb - 1
    r_lag = 2 * (nb - 1)

    def step(t, carry):
        @pl.when(chained & inside(t))
        def _():
            near_step(t)
        if lent:
            @pl.when(chained & helps & inside(t - 1) & is_lent(t - 1))
            def _():
                near_lent(t - 1)
        for j in range(nb):
            pass_on(n_all, n_send, n_recv, chained, t - j, j)
        kr = t - n_lag

        @pl.when(kr == 0)
        def _():
            for q in range(2):
                arrived(gl.at[q], gl_recv.at[q])
            take_weight(0)
        if lent:
            @pl.when((kr == 0) & is_end)
            def _():
                lend_own().start()

            @pl.when((kr == first_lent) & helps)
            def _():
                take_lent(0)

        @pl.when(inside(kr) & takes_part(kr))
        def _():
            reduced_step(kr)
        if lent:
            @pl.when(helps & inside(kr - 1) & is_lent(kr - 1))
            def _():
                reduced_lent(kr - 1)
        for j in range(nb):
            pass_on(r_all, r_send, r_recv, True, kr - j, j)

        for m in range(1, 3):
            @pl.when(kr == min(m, nch - 1))
            def _():
                take_weight(m)
        if lent:
            for m in range(3):
                @pl.when((t == m) & home & is_end)
                def _():
                    arrived(w.at[m, p], w_recv.at[m, p])
                    lend_weight(m, p).start()

                @pl.when((kr == m) & home & is_end)
                def _():
                    lend_weight(m, 1 - p).start()

                if m:
                    @pl.when((kr == first_lent + m) & helps)
                    def _():
                        take_lent(m)
        kf = t - r_lag

        @pl.when(inside(kf) & takes_part(kf))
        def _():
            final_step(kf)
        if lent:
            @pl.when(helps & inside(kf) & is_lent(kf))
            def _():
                final_lent(kf)
        ko = kf - 1

        @pl.when(inside(ko))
        def _():
            out_step(ko)
        return carry

    lax.fori_loop(0, nch + r_lag + 1, step, 0)

    def drain(k, carry):
        sent(n_all, n_send, n_recv, chained, k)
        sent(r_all, r_send, r_recv, True, k)
        for q in range(2):
            @pl.when((l >= 1) & jnp.logical_not(above_stays(q)))
            def _():
                above_copy(q, k).wait_send()

            @pl.when(takes_part(k) & jnp.logical_not(stays(q, role)))
            def _():
                local_copy(k, q).wait_send()

            @pl.when(takes_part(k) & chained & jnp.logical_not(stays(q, role + 1)))
            def _():
                push_copy(k, q).wait_send()

            if lent:
                @pl.when(is_lent(k) & helps)
                def _():
                    local_lent(k, q).wait_send()

                @pl.when(is_lent(k) & helps & chained)
                def _():
                    push_lent(k, q).wait_send()
        if lent:
            @pl.when(chained & jnp.logical_not(takes_part(k)))
            def _():
                lend_above(k).wait_send()
        return carry

    lax.fori_loop(0, nch, drain, 0)
    if lent:
        @pl.when(is_end)
        def _():
            lend_own().wait_send()
        for m in range(3):
            for q in range(2):
                @pl.when(home & is_end)
                def _():
                    lend_weight(m, q).wait_send()

                @pl.when(home & helps)
                def _():
                    share_weight(m, q).wait_send()

    @pl.when(home)
    def _():
        for i, src in enumerate((ps_ref, oi_ref)):
            remote(src.at[pl.ds((1 - c) * hb, hb)], tab.at[i], t_send.at[i], t_recv.at[i], core_mate).wait_send()
        remote(g_half(1 - c), gl.at[p], gl_send.at[0], gl_recv.at[p], core_mate).wait_send()
        for m in range(3):
            remote(w.at[m, 1 - p], w.at[m, 1 - p], w_fwd.at[m], w_recv.at[m, 1 - p], core_mate).wait_send()

    @pl.when(away)
    def _():
        remote(g_half(c), gl.at[p], gl_send.at[0], gl_recv.at[p], swap_mate).wait_send()
        remote(g_half(1 - c), gl.at[p], gl_send.at[1], gl_recv.at[p], swap_mate).wait_send()
    for m in range(3):
        remote(weights[m], w.at[m, p], w_send.at[m], w_recv.at[m, p], core_mate).wait_send()


def local(nl, nf, gradient, in_inverse, in_coupling, in_carry, out_inverse, out_coupling):
    g = gradient[0]
    r, d = g.shape
    nb = nf // 2
    blocks, blk = out_inverse.shape[1], out_inverse.shape[2]
    h = d // 2
    hb = blocks // 2
    nch = hb // 2 if hb % 2 == 0 else hb
    cw = h // nch
    lent = 2 if nb >= 4 and nch >= 5 else 0
    keep = max(lent, 1)
    dma = pltpu.SemaphoreType.DMA
    vm = pltpu.VMEM
    anyspec = pl.BlockSpec(memory_space=pl.ANY)
    out = pl.pallas_call(
        functools.partial(kernel, nl, nb, nch, lent),
        out_shape=jax.ShapeDtypeStruct((r, d), BF),
        in_specs=[anyspec] * 6,
        out_specs=pl.BlockSpec(memory_space=pltpu.VMEM),
        scratch_shapes=[
            vm((3, 2, r, d), BF), vm((2, r, h), BF), vm((nch, 2, r, cw), BF), vm((2, hb, blk, blk), BF),
            vm((nch, nb, 2 * r, cw), BF), vm((nch, nb, 2 * r, cw), BF),
            vm((nch, 2, r, cw), BF), vm((nch, 2, r, cw), BF), vm((nch, 2, r, cw), BF), vm((nch, 2, r, cw), BF),
            vm((3, 2, r, d), BF), vm((2, r, keep * cw), BF), vm((keep, 2, r, cw), BF),
            vm((keep, 2, r, cw), BF), vm((keep, 2, r, cw), BF),
            dma((3, 2)), dma((3,)), dma((3,)), dma((2,)), dma((2,)), dma((nch, 2)), dma((nch, 2)), dma((2,)), dma((2,)),
            dma((nch, nb)), dma((nch, nb, 2)), dma((nch, nb)), dma((nch, nb, 2)),
            dma((nch, 2)), dma((nch, 2)), dma((nch, 2)), dma((nch, 2)),
            dma((3, 2)), dma((3, 2)), dma((3, 2)), dma, dma, dma((keep,)), dma((keep,)), dma((keep, 2)), dma((keep, 2)),
        ],
        compiler_params=pltpu.CompilerParams(
            collective_id=0, has_side_effects=True, vmem_limit_bytes=62 * 1024 * 1024),
    )(g, in_inverse[0], in_coupling[0], in_carry[0], out_inverse[0], out_coupling[0])
    return out[None]


def solution(mesh):
    return jax.shard_map(
        functools.partial(local, mesh.shape["layer"], mesh.shape["feat"]),
        mesh=mesh,
        in_specs=(
            P("layer", "feat", None),
            P("layer", "feat", None),
            P("layer", "feat", None),
            P("layer", "feat", None),
            P("layer", None, None, None),
            P("layer", None, None, None),
        ),
        out_specs=P("layer", "feat", None),
        check_vma=False,
    )
```

```python
import functools

import jax
import jax.numpy as jnp
from jax import lax
from jax.experimental import pallas as pl
from jax.experimental.pallas import tpu as pltpu
from jax.sharding import PartitionSpec as P

MESH = pl.DeviceIdType.MESH
BF = jnp.bfloat16
F32 = jnp.float32


def kernel(nl, nb, nch, lent, g_ref, s_ref, c_ref, k_ref, oi_ref, ps_ref, out_ref,
           w, gl, gn, tab, n_all, r_all, l_st, p_st, l_in, p_in, w2, gl2, gn2, l_st2, p_st2,
           w_recv, w_send, w_fwd, gl_recv, gl_send, gn_recv, gn_send, t_recv, t_send,
           n_recv, n_send, r_recv, r_send, l_recv, l_send, p_recv, p_send,
           w2_recv, w2_send, w2_fwd, gl2_recv, gl2_send, gn2_recv, gn2_send, l2_send, p2_send):
    r, d = out_ref.shape
    h = d // 2
    cw = h // nch
    blk = ps_ref.shape[1]
    hb = ps_ref.shape[0] // 2
    per = cw // blk
    l = lax.axis_index("layer")
    f = lax.axis_index("feat")
    a, c = l // 2, l % 2
    b, p = f // 2, f % 2
    role = 2 * a + p
    home = c == p
    away = c != p
    chained = role < nl - 1
    core_mate = (2 * a + 1 - c, f)
    swap_mate = (l, 2 * b + 1 - p)

    def remote(src, dst, ss, rs, dev):
        return pltpu.make_async_remote_copy(
            src_ref=src, dst_ref=dst, send_sem=ss, recv_sem=rs,
            device_id=dev, device_id_type=MESH)

    def arrived(dst, sem):
        pltpu.make_async_copy(dst, dst, sem).wait()

    barrier = pltpu.get_barrier_semaphore()
    for dl in range(1, nl):
        for q in range(2):
            pl.semaphore_signal(barrier, inc=1, device_id=(lax.rem(l + dl, nl), 2 * b + q), device_id_type=MESH)
    pl.semaphore_signal(barrier, inc=1, device_id=swap_mate, device_id_type=MESH)

    first_lent = nch - lent
    is_end = (b == 0) | (b == nb - 1)
    helps = (b == 1) | (b == nb - 2)
    mate_b = jnp.where((b == 0) | (b == nb - 1), jnp.where(b == 0, 1, nb - 2), jnp.where(b == 1, 0, nb - 1))
    if not lent:
        is_end = helps = b < 0
    paired = is_end | helps

    def mate(layer, q):
        return (layer, 2 * mate_b + q)

    @pl.when(paired)
    def _():
        for dl in range(nl):
            for q in range(2):
                pl.semaphore_signal(barrier, inc=1, device_id=mate(dl, q), device_id_type=MESH)

    low_plain = (b > 0) & jnp.logical_not(paired & (mate_b == b - 1))
    high_plain = (b < nb - 1) & jnp.logical_not(paired & (mate_b == b + 1))

    @pl.when(low_plain)
    def _():
        pl.semaphore_signal(barrier, inc=1, device_id=(l, f - 2), device_id_type=MESH)

    @pl.when(high_plain)
    def _():
        pl.semaphore_signal(barrier, inc=1, device_id=(l, f + 2), device_id_type=MESH)

    peers = 2 * nl - 1 + jnp.where(paired, 2 * nl, 0) + jnp.where(low_plain, 1, 0) + jnp.where(high_plain, 1, 0)
    pl.semaphore_wait(barrier, peers)

    low = l + nl - 1
    low_a, low_p = (low - nl) // 2, lax.rem(low, 2)

    def above_cols(hh, k):
        return g_ref.at[:, pl.ds(pl.multiple_of(hh * h + k * cw, cw), cw)]

    def above_stays(hh):
        return (l >= 1) & (c == 1) & (p == 0) & (c == hh)

    def above_copy(hh, k):
        return remote(above_cols(hh, k), gn.at[k, p], gn_send.at[k, hh], gn_recv.at[k, p],
                      (2 * low_a + hh, 2 * b + low_p))

    def send_above(k, carry):
        for hh in range(2):
            @pl.when(above_stays(hh))
            def _():
                pltpu.make_async_copy(above_cols(hh, k), gn.at[k, p], gn_recv.at[k, p]).start()

            @pl.when((l >= 1) & jnp.logical_not(above_stays(hh)))
            def _():
                above_copy(hh, k).start()
        return carry

    lax.fori_loop(0, nch, send_above, 0)

    @pl.when(home)
    def _():
        pltpu.make_async_copy(ps_ref.at[pl.ds(c * hb, hb)], tab.at[0], t_recv.at[0]).start()
        pltpu.make_async_copy(oi_ref.at[pl.ds(c * hb, hb)], tab.at[1], t_recv.at[1]).start()
        remote(ps_ref.at[pl.ds((1 - c) * hb, hb)], tab.at[0], t_send.at[0], t_recv.at[0], core_mate).start()
        remote(oi_ref.at[pl.ds((1 - c) * hb, hb)], tab.at[1], t_send.at[1], t_recv.at[1], core_mate).start()

    def g_half(hh):
        return g_ref.at[:, pl.ds(pl.multiple_of(hh * h, 128), h)]

    @pl.when(home)
    def _():
        pltpu.make_async_copy(g_half(c), gl.at[p], gl_recv.at[p]).start()
        remote(g_half(1 - c), gl.at[p], gl_send.at[0], gl_recv.at[p], core_mate).start()

    @pl.when(away)
    def _():
        remote(g_half(c), gl.at[p], gl_send.at[0], gl_recv.at[p], swap_mate).start()
        remote(g_half(1 - c), gl.at[p], gl_send.at[1], gl_recv.at[p], (2 * a + 1 - c, 2 * b + 1 - p)).start()

    weights = (c_ref, s_ref, k_ref)
    for m in range(3):
        @pl.when(home)
        def _():
            pltpu.make_async_copy(weights[m], w.at[m, p], w_recv.at[m, p]).start()
            remote(weights[m], w.at[m, p], w_send.at[m], w_recv.at[m, p], core_mate).start()

        @pl.when(away)
        def _():
            remote(weights[m], w.at[m, p], w_send.at[m], w_recv.at[m, p], swap_mate).start()

    def take_weight(m):
        arrived(w.at[m, 1 - p], w_recv.at[m, 1 - p])

        @pl.when(home)
        def _():
            remote(w.at[m, 1 - p], w.at[m, 1 - p], w_fwd.at[m], w_recv.at[m, 1 - p], core_mate).start()
        waited = home & is_end

        @pl.when(jnp.logical_not(waited))
        def _():
            arrived(w.at[m, p], w_recv.at[m, p])

    def hop(buf, k, src, up, send, recv):
        dev = (l, f + 2) if up else (l, f - 2)
        return remote(buf.at[k, src], buf.at[k, src], send.at[k, src, 0 if up else 1], recv.at[k, src], dev)

    def is_lent(k):
        return k >= first_lent

    def takes_part(k):
        return jnp.logical_not(is_lent(k) & is_end)

    def goes_up(k):
        return (b < nb - 1) & takes_part(k) & jnp.logical_not(is_lent(k) & (b + 1 == nb - 1))

    def goes_down(k):
        return (b > 0) & takes_part(k) & jnp.logical_not(is_lent(k) & (b - 1 == 0))

    def made_here(k, src):
        return is_lent(k) & helps & (src == mate_b)

    def pass_on(buf, send, recv, live, k, j):
        ok = live & (k >= 0) & (k < nch) & takes_part(k)
        if j == 0:
            @pl.when(ok & goes_up(k))
            def _():
                hop(buf, k, b, True, send, recv).start()

            @pl.when(ok & goes_down(k))
            def _():
                hop(buf, k, b, False, send, recv).start()
        else:
            for src, there, onward, up in ((b - j, b - j >= 0, goes_up(k), True),
                                           (b + j, b + j < nb, goes_down(k), False)):
                @pl.when(ok & there & jnp.logical_not(made_here(k, src)))
                def _():
                    arrived(buf.at[k, src], recv.at[k, src])

                @pl.when(ok & there & onward)
                def _():
                    hop(buf, k, src, up, send, recv).start()

    def sent(buf, send, recv, live, k):
        for src in range(nb):
            @pl.when(live & (src <= b) & goes_up(k))
            def _():
                hop(buf, k, src, True, send, recv).wait_send()

            @pl.when(live & (src >= b) & goes_down(k))
            def _():
                hop(buf, k, src, False, send, recv).wait_send()

    def columns(k):
        return pl.ds(pl.multiple_of(k * cw, cw), cw)

    for i in range(2):
        arrived(tab.at[i], t_recv.at[i])

    def near_of(x, k):
        parts = [lax.dot_general(x[:, i * blk:(i + 1) * blk], tab[0, k * per + i],
                                 (((1,), (1,)), ((), ())), preferred_element_type=F32).astype(BF)
                 for i in range(per)]
        return jnp.concatenate(parts, axis=1)

    def lend_above(k):
        return remote(gn.at[k], gn2.at[k - first_lent], gn2_send.at[k - first_lent],
                      gn2_recv.at[k - first_lent], mate(l, p))

    def lend_own():
        cols = pl.ds(first_lent * cw, lent * cw)
        return remote(gl.at[:, :, cols], gl2, gl2_send, gl2_recv, mate(l, p))

    def lend_weight(m, q):
        return remote(w.at[m, q], w2.at[m, q], w2_send.at[m, q], w2_recv.at[m, q], mate(l, p))

    def share_weight(m, q):
        return remote(w2.at[m, q], w2.at[m, q], w2_fwd.at[m, q], w2_recv.at[m, q], core_mate)

    def take_lent(m):
        for q in range(2):
            arrived(w2.at[m, q], w2_recv.at[m, q])

            @pl.when(home)
            def _():
                share_weight(m, q).start()

    def near_step(k):
        for q in range(2):
            arrived(gn.at[k, q], gn_recv.at[k, q])

        @pl.when(takes_part(k))
        def _():
            n_all[k, b] = near_of(gn[k].reshape(2 * r, cw), k)

        if lent:
            @pl.when(jnp.logical_not(takes_part(k)))
            def _():
                lend_above(k).start()

    def near_lent(k):
        i = k - first_lent
        arrived(gn2.at[i], gn2_recv.at[i])
        n_all[k, mate_b] = near_of(gn2[i].reshape(2 * r, cw), k)

    def reduced_lent(k):
        cols = pl.ds(pl.multiple_of((k - first_lent) * cw, cw), cw)

        @pl.when(k == first_lent)
        def _():
            arrived(gl2, gl2_recv)

        @pl.when(chained)
        def _():
            x = n_all[k].reshape(nb * 2 * r, cw)
            coupled = jnp.dot(w2[0].reshape(2 * r, d), x, preferred_element_type=F32)
            r_all[k, mate_b] = (gl2[:, :, cols].reshape(2 * r, cw).astype(F32) - coupled).astype(BF)

        @pl.when(jnp.logical_not(chained))
        def _():
            r_all[k, mate_b] = gl2[:, :, cols].reshape(2 * r, cw)

    def local_lent(k, q):
        i = k - first_lent
        return remote(l_st2.at[i, q], l_in.at[k, c], l2_send.at[i, q], l_recv.at[k, c], mate(role, q))

    def push_lent(k, q):
        i = k - first_lent
        return remote(p_st2.at[i, q], p_in.at[k, c], p2_send.at[i, q], p_recv.at[k, c],
                      mate(lax.rem(role + 1, nl), q))

    def final_lent(k):
        i = k - first_lent
        x = r_all[k].reshape(nb * 2 * r, cw)
        white = jnp.dot(w2[1].reshape(2 * r, d), x, preferred_element_type=F32).astype(BF)
        for n in range(per):
            o = jnp.dot(white[:, n * blk:(n + 1) * blk], tab[1, k * per + n], preferred_element_type=F32)
            l_st2[i, :, :, n * blk:(n + 1) * blk] = o.astype(BF).reshape(2, r, blk)
        for q in range(2):
            local_lent(k, q).start()

        @pl.when(chained)
        def _():
            y = r_all[k].reshape(nb * 2 * r, cw)
            carried = jnp.dot(w2[2].reshape(2 * r, d), y, preferred_element_type=F32).astype(BF)
            for n in range(per):
                mid = jnp.dot(carried[:, n * blk:(n + 1) * blk], tab[1, k * per + n],
                              preferred_element_type=F32).astype(BF)
                o = jnp.dot(mid, tab[0, k * per + n], preferred_element_type=F32)
                p_st2[i, :, :, n * blk:(n + 1) * blk] = o.astype(BF).reshape(2, r, blk)
            for q in range(2):
                push_lent(k, q).start()

    def reduced_step(k):
        @pl.when(chained)
        def _():
            x = n_all[k].reshape(nb * 2 * r, cw)
            coupled = jnp.dot(w[0].reshape(2 * r, d), x, preferred_element_type=F32)
            g = gl[:, :, columns(k)].reshape(2 * r, cw).astype(F32)
            r_all[k, b] = (g - coupled).astype(BF)

        @pl.when(jnp.logical_not(chained))
        def _():
            r_all[k, b] = gl[:, :, columns(k)].reshape(2 * r, cw)

    def local_copy(k, q):
        return remote(l_st.at[k, q], l_in.at[k, c], l_send.at[k, q], l_recv.at[k, c], (role, 2 * b + q))

    def push_copy(k, q):
        return remote(p_st.at[k, q], p_in.at[k, c], p_send.at[k, q], p_recv.at[k, c],
                      (lax.rem(role + 1, nl), 2 * b + q))

    def stays(q, layer):
        return (l == layer) & (p == q)

    def final_step(k):
        x = r_all[k].reshape(nb * 2 * r, cw)
        white = jnp.dot(w[1].reshape(2 * r, d), x, preferred_element_type=F32).astype(BF)
        for i in range(per):
            o = jnp.dot(white[:, i * blk:(i + 1) * blk], tab[1, k * per + i], preferred_element_type=F32)
            l_st[k, :, :, i * blk:(i + 1) * blk] = o.astype(BF).reshape(2, r, blk)
        for q in range(2):
            @pl.when(stays(q, role))
            def _():
                pltpu.make_async_copy(l_st.at[k, q], l_in.at[k, c], l_recv.at[k, c]).start()

            @pl.when(jnp.logical_not(stays(q, role)))
            def _():
                local_copy(k, q).start()

        @pl.when(chained)
        def _():
            y = r_all[k].reshape(nb * 2 * r, cw)
            carried = jnp.dot(w[2].reshape(2 * r, d), y, preferred_element_type=F32).astype(BF)
            for i in range(per):
                mid = jnp.dot(carried[:, i * blk:(i + 1) * blk], tab[1, k * per + i],
                              preferred_element_type=F32).astype(BF)
                o = jnp.dot(mid, tab[0, k * per + i], preferred_element_type=F32)
                p_st[k, :, :, i * blk:(i + 1) * blk] = o.astype(BF).reshape(2, r, blk)
            for q in range(2):
                @pl.when(stays(q, role + 1))
                def _():
                    pltpu.make_async_copy(p_st.at[k, q], p_in.at[k, c], p_recv.at[k, c]).start()

                @pl.when(jnp.logical_not(stays(q, role + 1)))
                def _():
                    push_copy(k, q).start()

    def out_step(k):
        for hh in range(2):
            arrived(l_in.at[k, hh], l_recv.at[k, hh])
            dst = pl.ds(pl.multiple_of(hh * h + k * cw, cw), cw)

            @pl.when(l > 0)
            def _():
                arrived(p_in.at[k, hh], p_recv.at[k, hh])
                out_ref[:, dst] = (l_in[k, hh].astype(F32) - p_in[k, hh].astype(F32)).astype(BF)

            @pl.when(l == 0)
            def _():
                out_ref[:, dst] = l_in[k, hh]

    def inside(k):
        return (k >= 0) & (k < nch)

    n_lag = nb - 1
    r_lag = 2 * (nb - 1)

    def step(t, carry):
        @pl.when(chained & inside(t))
        def _():
            near_step(t)
        if lent:
            @pl.when(chained & helps & inside(t - 1) & is_lent(t - 1))
            def _():
                near_lent(t - 1)
        for j in range(nb):
            pass_on(n_all, n_send, n_recv, chained, t - j, j)
        kr = t - n_lag

        @pl.when(kr == 0)
        def _():
            for q in range(2):
                arrived(gl.at[q], gl_recv.at[q])
            take_weight(0)
        if lent:
            @pl.when((kr == 0) & is_end)
            def _():
                lend_own().start()

            @pl.when((kr == first_lent) & helps)
            def _():
                take_lent(0)

        @pl.when(inside(kr) & takes_part(kr))
        def _():
            reduced_step(kr)
        if lent:
            @pl.when(helps & inside(kr - 1) & is_lent(kr - 1))
            def _():
                reduced_lent(kr - 1)
        for j in range(nb):
            pass_on(r_all, r_send, r_recv, True, kr - j, j)

        if lent:
            for m in range(3):
                @pl.when((t == m + 2) & home & is_end)
                def _():
                    arrived(w.at[m, p], w_recv.at[m, p])
                    lend_weight(m, p).start()

                if m == 0:
                    @pl.when((kr == 0) & home & is_end)
                    def _():
                        lend_weight(m, 1 - p).start()
        kf = t - r_lag

        @pl.when(kf == 0)
        def _():
            take_weight(1)
            take_weight(2)
        if lent:
            for m in range(1, 3):
                @pl.when((kf == 0) & home & is_end)
                def _():
                    lend_weight(m, 1 - p).start()

                @pl.when((kf == first_lent) & helps)
                def _():
                    take_lent(m)

        @pl.when(inside(kf) & takes_part(kf))
        def _():
            final_step(kf)
        if lent:
            @pl.when(helps & inside(kf) & is_lent(kf))
            def _():
                final_lent(kf)
        ko = kf - 1

        @pl.when(inside(ko))
        def _():
            out_step(ko)
        return carry

    lax.fori_loop(0, nch + r_lag + 1, step, 0)

    def drain(k, carry):
        sent(n_all, n_send, n_recv, chained, k)
        sent(r_all, r_send, r_recv, True, k)
        for q in range(2):
            @pl.when((l >= 1) & jnp.logical_not(above_stays(q)))
            def _():
                above_copy(q, k).wait_send()

            @pl.when(takes_part(k) & jnp.logical_not(stays(q, role)))
            def _():
                local_copy(k, q).wait_send()

            @pl.when(takes_part(k) & chained & jnp.logical_not(stays(q, role + 1)))
            def _():
                push_copy(k, q).wait_send()

            if lent:
                @pl.when(is_lent(k) & helps)
                def _():
                    local_lent(k, q).wait_send()

                @pl.when(is_lent(k) & helps & chained)
                def _():
                    push_lent(k, q).wait_send()
        if lent:
            @pl.when(chained & jnp.logical_not(takes_part(k)))
            def _():
                lend_above(k).wait_send()
        return carry

    lax.fori_loop(0, nch, drain, 0)
    if lent:
        @pl.when(is_end)
        def _():
            lend_own().wait_send()
        for m in range(3):
            for q in range(2):
                @pl.when(home & is_end)
                def _():
                    lend_weight(m, q).wait_send()

                @pl.when(home & helps)
                def _():
                    share_weight(m, q).wait_send()

    @pl.when(home)
    def _():
        for i, src in enumerate((ps_ref, oi_ref)):
            remote(src.at[pl.ds((1 - c) * hb, hb)], tab.at[i], t_send.at[i], t_recv.at[i], core_mate).wait_send()
        remote(g_half(1 - c), gl.at[p], gl_send.at[0], gl_recv.at[p], core_mate).wait_send()
        for m in range(3):
            remote(w.at[m, 1 - p], w.at[m, 1 - p], w_fwd.at[m], w_recv.at[m, 1 - p], core_mate).wait_send()

    @pl.when(away)
    def _():
        remote(g_half(c), gl.at[p], gl_send.at[0], gl_recv.at[p], swap_mate).wait_send()
        remote(g_half(1 - c), gl.at[p], gl_send.at[1], gl_recv.at[p], swap_mate).wait_send()
    for m in range(3):
        remote(weights[m], w.at[m, p], w_send.at[m], w_recv.at[m, p], core_mate).wait_send()


def local(nl, nf, gradient, in_inverse, in_coupling, in_carry, out_inverse, out_coupling):
    g = gradient[0]
    r, d = g.shape
    nb = nf // 2
    blocks, blk = out_inverse.shape[1], out_inverse.shape[2]
    h = d // 2
    hb = blocks // 2
    nch = hb // 2 if hb % 2 == 0 else hb
    cw = h // nch
    lent = 1 if nb >= 4 and nch >= 5 else 0
    keep = max(lent, 1)
    dma = pltpu.SemaphoreType.DMA
    vm = pltpu.VMEM
    anyspec = pl.BlockSpec(memory_space=pl.ANY)
    out = pl.pallas_call(
        functools.partial(kernel, nl, nb, nch, lent),
        out_shape=jax.ShapeDtypeStruct((r, d), BF),
        in_specs=[anyspec] * 6,
        out_specs=pl.BlockSpec(memory_space=pltpu.VMEM),
        scratch_shapes=[
            vm((3, 2, r, d), BF), vm((2, r, h), BF), vm((nch, 2, r, cw), BF), vm((2, hb, blk, blk), BF),
            vm((nch, nb, 2 * r, cw), BF), vm((nch, nb, 2 * r, cw), BF),
            vm((nch, 2, r, cw), BF), vm((nch, 2, r, cw), BF), vm((nch, 2, r, cw), BF), vm((nch, 2, r, cw), BF),
            vm((3, 2, r, d), BF), vm((2, r, keep * cw), BF), vm((keep, 2, r, cw), BF),
            vm((keep, 2, r, cw), BF), vm((keep, 2, r, cw), BF),
            dma((3, 2)), dma((3,)), dma((3,)), dma((2,)), dma((2,)), dma((nch, 2)), dma((nch, 2)), dma((2,)), dma((2,)),
            dma((nch, nb)), dma((nch, nb, 2)), dma((nch, nb)), dma((nch, nb, 2)),
            dma((nch, 2)), dma((nch, 2)), dma((nch, 2)), dma((nch, 2)),
            dma((3, 2)), dma((3, 2)), dma((3, 2)), dma, dma, dma((keep,)), dma((keep,)), dma((keep, 2)), dma((keep, 2)),
        ],
        compiler_params=pltpu.CompilerParams(
            collective_id=0, has_side_effects=True, vmem_limit_bytes=62 * 1024 * 1024),
    )(g, in_inverse[0], in_coupling[0], in_carry[0], out_inverse[0], out_coupling[0])
    return out[None]


def solution(mesh):
    return jax.shard_map(
        functools.partial(local, mesh.shape["layer"], mesh.shape["feat"]),
        mesh=mesh,
        in_specs=(
            P("layer", "feat", None),
            P("layer", "feat", None),
            P("layer", "feat", None),
            P("layer", "feat", None),
            P("layer", None, None, None),
            P("layer", None, None, None),
        ),
        out_specs=P("layer", "feat", None),
        check_vma=False,
    )
```

```python
import functools

import jax
import jax.numpy as jnp
from jax import lax
from jax.experimental import pallas as pl
from jax.experimental.pallas import tpu as pltpu
from jax.sharding import PartitionSpec as P

MESH = pl.DeviceIdType.MESH
BF = jnp.bfloat16
F32 = jnp.float32


def kernel(nl, nb, nch, lent, g_ref, s_ref, c_ref, k_ref, oi_ref, ps_ref, out_ref,
           w, gl, gn, tab, n_all, r_all, l_st, p_st, l_in, p_in, w2, gl2, gn2, l_st2, p_st2,
           w_recv, w_send, w_fwd, gl_recv, gl_send, gn_recv, gn_send, t_recv, t_send,
           n_recv, n_send, r_recv, r_send, l_recv, l_send, p_recv, p_send,
           w2_recv, w2_send, w2_fwd, gl2_recv, gl2_send, gn2_recv, gn2_send, l2_send, p2_send):
    r, d = out_ref.shape
    h = d // 2
    cw = h // nch
    blk = ps_ref.shape[1]
    hb = ps_ref.shape[0] // 2
    per = cw // blk
    l = lax.axis_index("layer")
    f = lax.axis_index("feat")
    a, c = l // 2, l % 2
    b, p = f // 2, f % 2
    role = 2 * a + p
    home = c == p
    away = c != p
    chained = role < nl - 1
    core_mate = (2 * a + 1 - c, f)
    swap_mate = (l, 2 * b + 1 - p)

    def remote(src, dst, ss, rs, dev):
        return pltpu.make_async_remote_copy(
            src_ref=src, dst_ref=dst, send_sem=ss, recv_sem=rs,
            device_id=dev, device_id_type=MESH)

    def arrived(dst, sem):
        pltpu.make_async_copy(dst, dst, sem).wait()

    barrier = pltpu.get_barrier_semaphore()
    for dl in range(1, nl):
        for q in range(2):
            pl.semaphore_signal(barrier, inc=1, device_id=(lax.rem(l + dl, nl), 2 * b + q), device_id_type=MESH)
    pl.semaphore_signal(barrier, inc=1, device_id=swap_mate, device_id_type=MESH)

    first_lent = nch - lent
    is_end = (b == 0) | (b == nb - 1)
    helps = (b == 1) | (b == nb - 2)
    mate_b = jnp.where((b == 0) | (b == nb - 1), jnp.where(b == 0, 1, nb - 2), jnp.where(b == 1, 0, nb - 1))
    if not lent:
        is_end = helps = b < 0
    paired = is_end | helps

    def mate(layer, q):
        return (layer, 2 * mate_b + q)

    @pl.when(paired)
    def _():
        for dl in range(nl):
            for q in range(2):
                pl.semaphore_signal(barrier, inc=1, device_id=mate(dl, q), device_id_type=MESH)

    low_plain = (b > 0) & jnp.logical_not(paired & (mate_b == b - 1))
    high_plain = (b < nb - 1) & jnp.logical_not(paired & (mate_b == b + 1))

    @pl.when(low_plain)
    def _():
        pl.semaphore_signal(barrier, inc=1, device_id=(l, f - 2), device_id_type=MESH)

    @pl.when(high_plain)
    def _():
        pl.semaphore_signal(barrier, inc=1, device_id=(l, f + 2), device_id_type=MESH)

    peers = 2 * nl - 1 + jnp.where(paired, 2 * nl, 0) + jnp.where(low_plain, 1, 0) + jnp.where(high_plain, 1, 0)
    pl.semaphore_wait(barrier, peers)

    low = l + nl - 1
    low_a, low_p = (low - nl) // 2, lax.rem(low, 2)

    def above_cols(hh, k):
        return g_ref.at[:, pl.ds(pl.multiple_of(hh * h + k * cw, cw), cw)]

    def above_stays(hh):
        return (l >= 1) & (c == 1) & (p == 0) & (c == hh)

    def above_copy(hh, k):
        return remote(above_cols(hh, k), gn.at[k, p], gn_send.at[k, hh], gn_recv.at[k, p],
                      (2 * low_a + hh, 2 * b + low_p))

    def send_above(k, carry):
        for hh in range(2):
            @pl.when(above_stays(hh))
            def _():
                pltpu.make_async_copy(above_cols(hh, k), gn.at[k, p], gn_recv.at[k, p]).start()

            @pl.when((l >= 1) & jnp.logical_not(above_stays(hh)))
            def _():
                above_copy(hh, k).start()
        return carry

    lax.fori_loop(0, nch, send_above, 0)

    @pl.when(home)
    def _():
        pltpu.make_async_copy(ps_ref.at[pl.ds(c * hb, hb)], tab.at[0], t_recv.at[0]).start()
        pltpu.make_async_copy(oi_ref.at[pl.ds(c * hb, hb)], tab.at[1], t_recv.at[1]).start()
        remote(ps_ref.at[pl.ds((1 - c) * hb, hb)], tab.at[0], t_send.at[0], t_recv.at[0], core_mate).start()
        remote(oi_ref.at[pl.ds((1 - c) * hb, hb)], tab.at[1], t_send.at[1], t_recv.at[1], core_mate).start()

    def g_half(hh):
        return g_ref.at[:, pl.ds(pl.multiple_of(hh * h, 128), h)]

    @pl.when(home)
    def _():
        pltpu.make_async_copy(g_half(c), gl.at[p], gl_recv.at[p]).start()
        remote(g_half(1 - c), gl.at[p], gl_send.at[0], gl_recv.at[p], core_mate).start()

    @pl.when(away)
    def _():
        remote(g_half(c), gl.at[p], gl_send.at[0], gl_recv.at[p], swap_mate).start()
        remote(g_half(1 - c), gl.at[p], gl_send.at[1], gl_recv.at[p], (2 * a + 1 - c, 2 * b + 1 - p)).start()

    weights = (c_ref, s_ref, k_ref)
    for m in range(3):
        @pl.when(home)
        def _():
            pltpu.make_async_copy(weights[m], w.at[m, p], w_recv.at[m, p]).start()
            remote(weights[m], w.at[m, p], w_send.at[m], w_recv.at[m, p], core_mate).start()

        @pl.when(away)
        def _():
            remote(weights[m], w.at[m, p], w_send.at[m], w_recv.at[m, p], swap_mate).start()

    def take_weight(m):
        arrived(w.at[m, 1 - p], w_recv.at[m, 1 - p])

        @pl.when(home)
        def _():
            remote(w.at[m, 1 - p], w.at[m, 1 - p], w_fwd.at[m], w_recv.at[m, 1 - p], core_mate).start()
        waited = home & is_end

        @pl.when(jnp.logical_not(waited))
        def _():
            arrived(w.at[m, p], w_recv.at[m, p])

    def hop(buf, k, src, up, send, recv):
        dev = (l, f + 2) if up else (l, f - 2)
        return remote(buf.at[k, src], buf.at[k, src], send.at[k, src, 0 if up else 1], recv.at[k, src], dev)

    def is_lent(k):
        return k >= first_lent

    def takes_part(k):
        return jnp.logical_not(is_lent(k) & is_end)

    def goes_up(k):
        return (b < nb - 1) & takes_part(k) & jnp.logical_not(is_lent(k) & (b + 1 == nb - 1))

    def goes_down(k):
        return (b > 0) & takes_part(k) & jnp.logical_not(is_lent(k) & (b - 1 == 0))

    def made_here(k, src):
        return is_lent(k) & helps & (src == mate_b)

    def pass_on(buf, send, recv, live, k, j):
        ok = live & (k >= 0) & (k < nch) & takes_part(k)
        if j == 0:
            @pl.when(ok & goes_up(k))
            def _():
                hop(buf, k, b, True, send, recv).start()

            @pl.when(ok & goes_down(k))
            def _():
                hop(buf, k, b, False, send, recv).start()
        else:
            for src, there, onward, up in ((b - j, b - j >= 0, goes_up(k), True),
                                           (b + j, b + j < nb, goes_down(k), False)):
                @pl.when(ok & there & jnp.logical_not(made_here(k, src)))
                def _():
                    arrived(buf.at[k, src], recv.at[k, src])

                @pl.when(ok & there & onward)
                def _():
                    hop(buf, k, src, up, send, recv).start()

    def sent(buf, send, recv, live, k):
        for src in range(nb):
            @pl.when(live & (src <= b) & goes_up(k))
            def _():
                hop(buf, k, src, True, send, recv).wait_send()

            @pl.when(live & (src >= b) & goes_down(k))
            def _():
                hop(buf, k, src, False, send, recv).wait_send()

    def columns(k):
        return pl.ds(pl.multiple_of(k * cw, cw), cw)

    for i in range(2):
        arrived(tab.at[i], t_recv.at[i])

    def near_of(x, k):
        parts = [lax.dot_general(x[:, i * blk:(i + 1) * blk], tab[0, k * per + i],
                                 (((1,), (1,)), ((), ())), preferred_element_type=F32).astype(BF)
                 for i in range(per)]
        return jnp.concatenate(parts, axis=1)

    def lend_above(k):
        return remote(gn.at[k], gn2.at[k - first_lent], gn2_send.at[k - first_lent],
                      gn2_recv.at[k - first_lent], mate(l, p))

    def lend_own():
        cols = pl.ds(first_lent * cw, lent * cw)
        return remote(gl.at[:, :, cols], gl2, gl2_send, gl2_recv, mate(l, p))

    def lend_weight(m, q):
        return remote(w.at[m, q], w2.at[m, q], w2_send.at[m, q], w2_recv.at[m, q], mate(l, p))

    def share_weight(m, q):
        return remote(w2.at[m, q], w2.at[m, q], w2_fwd.at[m, q], w2_recv.at[m, q], core_mate)

    def take_lent(m):
        for q in range(2):
            arrived(w2.at[m, q], w2_recv.at[m, q])

            @pl.when(home)
            def _():
                share_weight(m, q).start()

    def near_step(k):
        for q in range(2):
            arrived(gn.at[k, q], gn_recv.at[k, q])

        @pl.when(takes_part(k))
        def _():
            n_all[k, b] = near_of(gn[k].reshape(2 * r, cw), k)

        if lent:
            @pl.when(jnp.logical_not(takes_part(k)))
            def _():
                lend_above(k).start()

    def near_lent(k):
        i = k - first_lent
        arrived(gn2.at[i], gn2_recv.at[i])
        n_all[k, mate_b] = near_of(gn2[i].reshape(2 * r, cw), k)

    def reduced_lent(k):
        cols = pl.ds(pl.multiple_of((k - first_lent) * cw, cw), cw)

        @pl.when(k == first_lent)
        def _():
            arrived(gl2, gl2_recv)

        @pl.when(chained)
        def _():
            x = n_all[k].reshape(nb * 2 * r, cw)
            coupled = jnp.dot(w2[0].reshape(2 * r, d), x, preferred_element_type=F32)
            r_all[k, mate_b] = (gl2[:, :, cols].reshape(2 * r, cw).astype(F32) - coupled).astype(BF)

        @pl.when(jnp.logical_not(chained))
        def _():
            r_all[k, mate_b] = gl2[:, :, cols].reshape(2 * r, cw)

    def local_lent(k, q):
        i = k - first_lent
        return remote(l_st2.at[i, q], l_in.at[k, c], l2_send.at[i, q], l_recv.at[k, c], mate(role, q))

    def push_lent(k, q):
        i = k - first_lent
        return remote(p_st2.at[i, q], p_in.at[k, c], p2_send.at[i, q], p_recv.at[k, c],
                      mate(lax.rem(role + 1, nl), q))

    def final_lent(k):
        i = k - first_lent
        x = r_all[k].reshape(nb * 2 * r, cw)
        white = jnp.dot(w2[1].reshape(2 * r, d), x, preferred_element_type=F32).astype(BF)
        for n in range(per):
            o = jnp.dot(white[:, n * blk:(n + 1) * blk], tab[1, k * per + n], preferred_element_type=F32)
            l_st2[i, :, :, n * blk:(n + 1) * blk] = o.astype(BF).reshape(2, r, blk)
        for q in range(2):
            local_lent(k, q).start()

        @pl.when(chained)
        def _():
            y = r_all[k].reshape(nb * 2 * r, cw)
            carried = jnp.dot(w2[2].reshape(2 * r, d), y, preferred_element_type=F32).astype(BF)
            for n in range(per):
                mid = jnp.dot(carried[:, n * blk:(n + 1) * blk], tab[1, k * per + n],
                              preferred_element_type=F32).astype(BF)
                o = jnp.dot(mid, tab[0, k * per + n], preferred_element_type=F32)
                p_st2[i, :, :, n * blk:(n + 1) * blk] = o.astype(BF).reshape(2, r, blk)
            for q in range(2):
                push_lent(k, q).start()

    def reduced_step(k):
        @pl.when(chained)
        def _():
            x = n_all[k].reshape(nb * 2 * r, cw)
            coupled = jnp.dot(w[0].reshape(2 * r, d), x, preferred_element_type=F32)
            g = gl[:, :, columns(k)].reshape(2 * r, cw).astype(F32)
            r_all[k, b] = (g - coupled).astype(BF)

        @pl.when(jnp.logical_not(chained))
        def _():
            r_all[k, b] = gl[:, :, columns(k)].reshape(2 * r, cw)

    def local_copy(k, q):
        return remote(l_st.at[k, q], l_in.at[k, c], l_send.at[k, q], l_recv.at[k, c], (role, 2 * b + q))

    def push_copy(k, q):
        return remote(p_st.at[k, q], p_in.at[k, c], p_send.at[k, q], p_recv.at[k, c],
                      (lax.rem(role + 1, nl), 2 * b + q))

    def stays(q, layer):
        return (l == layer) & (p == q)

    def final_step(k):
        x = r_all[k].reshape(nb * 2 * r, cw)
        white = jnp.dot(w[1].reshape(2 * r, d), x, preferred_element_type=F32).astype(BF)
        for i in range(per):
            o = jnp.dot(white[:, i * blk:(i + 1) * blk], tab[1, k * per + i], preferred_element_type=F32)
            l_st[k, :, :, i * blk:(i + 1) * blk] = o.astype(BF).reshape(2, r, blk)
        for q in range(2):
            @pl.when(stays(q, role))
            def _():
                pltpu.make_async_copy(l_st.at[k, q], l_in.at[k, c], l_recv.at[k, c]).start()

            @pl.when(jnp.logical_not(stays(q, role)))
            def _():
                local_copy(k, q).start()

        @pl.when(chained)
        def _():
            y = r_all[k].reshape(nb * 2 * r, cw)
            carried = jnp.dot(w[2].reshape(2 * r, d), y, preferred_element_type=F32).astype(BF)
            for i in range(per):
                mid = jnp.dot(carried[:, i * blk:(i + 1) * blk], tab[1, k * per + i],
                              preferred_element_type=F32).astype(BF)
                o = jnp.dot(mid, tab[0, k * per + i], preferred_element_type=F32)
                p_st[k, :, :, i * blk:(i + 1) * blk] = o.astype(BF).reshape(2, r, blk)
            for q in range(2):
                @pl.when(stays(q, role + 1))
                def _():
                    pltpu.make_async_copy(p_st.at[k, q], p_in.at[k, c], p_recv.at[k, c]).start()

                @pl.when(jnp.logical_not(stays(q, role + 1)))
                def _():
                    push_copy(k, q).start()

    def out_step(k):
        for hh in range(2):
            arrived(l_in.at[k, hh], l_recv.at[k, hh])
            dst = pl.ds(pl.multiple_of(hh * h + k * cw, cw), cw)

            @pl.when(l > 0)
            def _():
                arrived(p_in.at[k, hh], p_recv.at[k, hh])
                out_ref[:, dst] = (l_in[k, hh].astype(F32) - p_in[k, hh].astype(F32)).astype(BF)

            @pl.when(l == 0)
            def _():
                out_ref[:, dst] = l_in[k, hh]

    def inside(k):
        return (k >= 0) & (k < nch)

    n_lag = nb - 1
    r_lag = 2 * (nb - 1)

    def step(t, carry):
        @pl.when(chained & inside(t))
        def _():
            near_step(t)
        if lent:
            @pl.when(chained & helps & inside(t - 1) & is_lent(t - 1))
            def _():
                near_lent(t - 1)
        for j in range(nb):
            pass_on(n_all, n_send, n_recv, chained, t - j, j)
        kr = t - n_lag

        @pl.when(kr == 0)
        def _():
            for q in range(2):
                arrived(gl.at[q], gl_recv.at[q])
            take_weight(0)
        if lent:
            @pl.when((kr == 0) & is_end)
            def _():
                lend_own().start()

            @pl.when((kr == first_lent) & helps)
            def _():
                take_lent(0)

        @pl.when(inside(kr) & takes_part(kr))
        def _():
            reduced_step(kr)
        if lent:
            @pl.when(helps & inside(kr - 1) & is_lent(kr - 1))
            def _():
                reduced_lent(kr - 1)
        for j in range(nb):
            pass_on(r_all, r_send, r_recv, True, kr - j, j)

        if lent:
            for m in range(3):
                @pl.when((t == m + 2) & home & is_end)
                def _():
                    arrived(w.at[m, p], w_recv.at[m, p])
                    lend_weight(m, p).start()

                if m == 0:
                    @pl.when((kr == 0) & home & is_end)
                    def _():
                        lend_weight(m, 1 - p).start()
        kf = t - r_lag

        @pl.when(kf == 0)
        def _():
            take_weight(1)
            take_weight(2)
        if lent:
            for m in range(1, 3):
                @pl.when((kf == 0) & home & is_end)
                def _():
                    lend_weight(m, 1 - p).start()

                @pl.when((kf == first_lent) & helps)
                def _():
                    take_lent(m)

        if lent:
            @pl.when(helps & inside(kf) & is_lent(kf))
            def _():
                final_lent(kf)

        @pl.when(inside(kf) & takes_part(kf))
        def _():
            final_step(kf)
        ko = kf - 1

        @pl.when(inside(ko))
        def _():
            out_step(ko)
        return carry

    lax.fori_loop(0, nch + r_lag + 1, step, 0)

    def drain(k, carry):
        sent(n_all, n_send, n_recv, chained, k)
        sent(r_all, r_send, r_recv, True, k)
        for q in range(2):
            @pl.when((l >= 1) & jnp.logical_not(above_stays(q)))
            def _():
                above_copy(q, k).wait_send()

            @pl.when(takes_part(k) & jnp.logical_not(stays(q, role)))
            def _():
                local_copy(k, q).wait_send()

            @pl.when(takes_part(k) & chained & jnp.logical_not(stays(q, role + 1)))
            def _():
                push_copy(k, q).wait_send()

            if lent:
                @pl.when(is_lent(k) & helps)
                def _():
                    local_lent(k, q).wait_send()

                @pl.when(is_lent(k) & helps & chained)
                def _():
                    push_lent(k, q).wait_send()
        if lent:
            @pl.when(chained & jnp.logical_not(takes_part(k)))
            def _():
                lend_above(k).wait_send()
        return carry

    lax.fori_loop(0, nch, drain, 0)
    if lent:
        @pl.when(is_end)
        def _():
            lend_own().wait_send()
        for m in range(3):
            for q in range(2):
                @pl.when(home & is_end)
                def _():
                    lend_weight(m, q).wait_send()

                @pl.when(home & helps)
                def _():
                    share_weight(m, q).wait_send()

    @pl.when(home)
    def _():
        for i, src in enumerate((ps_ref, oi_ref)):
            remote(src.at[pl.ds((1 - c) * hb, hb)], tab.at[i], t_send.at[i], t_recv.at[i], core_mate).wait_send()
        remote(g_half(1 - c), gl.at[p], gl_send.at[0], gl_recv.at[p], core_mate).wait_send()
        for m in range(3):
            remote(w.at[m, 1 - p], w.at[m, 1 - p], w_fwd.at[m], w_recv.at[m, 1 - p], core_mate).wait_send()

    @pl.when(away)
    def _():
        remote(g_half(c), gl.at[p], gl_send.at[0], gl_recv.at[p], swap_mate).wait_send()
        remote(g_half(1 - c), gl.at[p], gl_send.at[1], gl_recv.at[p], swap_mate).wait_send()
    for m in range(3):
        remote(weights[m], w.at[m, p], w_send.at[m], w_recv.at[m, p], core_mate).wait_send()


def local(nl, nf, gradient, in_inverse, in_coupling, in_carry, out_inverse, out_coupling):
    g = gradient[0]
    r, d = g.shape
    nb = nf // 2
    blocks, blk = out_inverse.shape[1], out_inverse.shape[2]
    h = d // 2
    hb = blocks // 2
    nch = hb // 2 if hb % 2 == 0 else hb
    cw = h // nch
    lent = 1 if nb >= 4 and nch >= 5 else 0
    keep = max(lent, 1)
    dma = pltpu.SemaphoreType.DMA
    vm = pltpu.VMEM
    anyspec = pl.BlockSpec(memory_space=pl.ANY)
    out = pl.pallas_call(
        functools.partial(kernel, nl, nb, nch, lent),
        out_shape=jax.ShapeDtypeStruct((r, d), BF),
        in_specs=[anyspec] * 6,
        out_specs=pl.BlockSpec(memory_space=pltpu.VMEM),
        scratch_shapes=[
            vm((3, 2, r, d), BF), vm((2, r, h), BF), vm((nch, 2, r, cw), BF), vm((2, hb, blk, blk), BF),
            vm((nch, nb, 2 * r, cw), BF), vm((nch, nb, 2 * r, cw), BF),
            vm((nch, 2, r, cw), BF), vm((nch, 2, r, cw), BF), vm((nch, 2, r, cw), BF), vm((nch, 2, r, cw), BF),
            vm((3, 2, r, d), BF), vm((2, r, keep * cw), BF), vm((keep, 2, r, cw), BF),
            vm((keep, 2, r, cw), BF), vm((keep, 2, r, cw), BF),
            dma((3, 2)), dma((3,)), dma((3,)), dma((2,)), dma((2,)), dma((nch, 2)), dma((nch, 2)), dma((2,)), dma((2,)),
            dma((nch, nb)), dma((nch, nb, 2)), dma((nch, nb)), dma((nch, nb, 2)),
            dma((nch, 2)), dma((nch, 2)), dma((nch, 2)), dma((nch, 2)),
            dma((3, 2)), dma((3, 2)), dma((3, 2)), dma, dma, dma((keep,)), dma((keep,)), dma((keep, 2)), dma((keep, 2)),
        ],
        compiler_params=pltpu.CompilerParams(
            collective_id=0, has_side_effects=True, vmem_limit_bytes=62 * 1024 * 1024),
    )(g, in_inverse[0], in_coupling[0], in_carry[0], out_inverse[0], out_coupling[0])
    return out[None]


def solution(mesh):
    return jax.shard_map(
        functools.partial(local, mesh.shape["layer"], mesh.shape["feat"]),
        mesh=mesh,
        in_specs=(
            P("layer", "feat", None),
            P("layer", "feat", None),
            P("layer", "feat", None),
            P("layer", "feat", None),
            P("layer", None, None, None),
            P("layer", None, None, None),
        ),
        out_specs=P("layer", "feat", None),
        check_vma=False,
    )
```
